32 devices in a mesh: row: 4 (over z), col: 8 (over y, x, core).
Axes of the slice: x: 2, y: 2, z: 4, core: 2. Of those that a mesh axis runs over, the one named last changes fastest.
Arguments:
- amplitudes: bfloat16 [16, 16, 12, 4096], P('row', 'col'), may hold values from -6 to 6
- integrals: bfloat16 [16, 16, 47, 4096], P('row', 'col'), may hold values from -0.1875 to 0.1875
- pair_lists: int32 [4, 12, 2], replicated, may hold values from 0 to 46, as said below
- tile_counts: int32 [4], replicated, may hold values from 1 to 12, as said below
Outputs:
- symmetric: float32 [16, 16, 12, 4096], P('row', 'col')
The draws below stay inside these ranges and needn't reach their ends.
Inputs may be any that keep to these rules, and one draw needn't show every extreme that they name: `pair_lists`: each grid row lists 12 distinct ordered pairs of different tiles. `tile_counts`: the largest count equals 12.
All inputs are finite; a program needn't handle non-finite values.
Results may differ from the reference program's by a relative error of at most 0.0029.
Values may be sent and summed in bfloat16 or wider, within the bound.
No kernel may reach another device: no remote copies, remote signals or barrier semaphores. Data moves between devices by JAX's collectives and lax.ppermute only.
A program may use at most 128 MiB of HBM per device.

```python
import jax
import jax.numpy as jnp
import numpy as np
from jax import lax

TILE = 64
NVT = 47
NP = 12
NOCC = 16
N_ROW = 4


def make_lists(key):
    upper_rows, upper_cols = np.triu_indices(NVT, 1)
    pair_table = jnp.asarray(np.stack([upper_rows, upper_cols], 1).astype(np.int32))
    table_size = pair_table.shape[0]
    forced_index = NVT - 2
    shuffled = jax.random.permutation(jax.random.fold_in(key, 11), table_size).astype(jnp.int32)
    ranking = jnp.where(jnp.arange(table_size, dtype=jnp.int32) == forced_index, -1, shuffled)
    chosen = jnp.argsort(ranking, stable=True)[:NP]
    base_pairs = pair_table[chosen]
    flips = jax.random.randint(jax.random.fold_in(key, 12), (N_ROW, NP, 1), 0, 2)
    oriented = jnp.where(flips == 1, base_pairs[None, :, ::-1], base_pairs[None, :, :])
    row_keys = jax.random.split(jax.random.fold_in(key, 15), N_ROW)
    orders = jax.vmap(lambda row_key: jax.random.permutation(row_key, NP))(row_keys)
    lists = jnp.take_along_axis(oriented, orders[:, :, None], axis=1).astype(jnp.int32)
    counts = jax.random.randint(jax.random.fold_in(key, 13), (N_ROW,), 1, NP + 1)
    full_row = jax.random.randint(jax.random.fold_in(key, 14), (), 0, N_ROW)
    counts = counts.at[full_row].set(NP).astype(jnp.int32)
    return (lists, counts)


def draw_pair_lists(key, part):
    return make_lists(key)[0]


def draw_tile_counts(key, part):
    return make_lists(key)[1]


def block_levels(rng, dims, pieces, low, high):
    def one(axis_at, shards_of):
        draws = jax.random.uniform(jax.random.fold_in(jax.random.fold_in(rng, 6), axis_at), (shards_of,), jnp.float32, low / len(pieces), high / len(pieces))
        return jnp.repeat(jnp.exp(draws), dims[axis_at] // shards_of).reshape((-1,) + (1,) * (len(dims) - axis_at - 1))

    level = one(*pieces[0])
    for cut in pieces[1:]:
        level = level * one(*cut)
    return level


def scatter_about(rng, dims, spread, limit, cuts=(), kind=jnp.bfloat16):
    result = jax.random.normal(rng, dims, jnp.float32) * spread
    if len(cuts) > 0:
        result = block_levels(rng, dims, cuts, -0.22, 0.18) * result
    return jnp.clip(result, min=-limit, max=limit).astype(kind)


def setup_inputs(seed: int = 0) -> dict:
    key_of = jax.random.split(jax.random.key(seed), 5)
    return {
        "amplitudes": scatter_about(key_of[0], (NOCC, NOCC, NP, TILE * TILE), 1.0, 6.0, ((0, 4), (1, 8))),
        "integrals": scatter_about(key_of[1], (NOCC, NOCC, NVT, TILE * TILE), (NOCC * TILE) ** -0.5, 0.1875, ((0, 4), (1, 8))),
        "pair_lists": draw_pair_lists(jax.random.fold_in(key_of[4], 71), 0),
        "tile_counts": draw_tile_counts(jax.random.fold_in(key_of[4], 71), 0),
    }


def reference(amplitudes, integrals, pair_lists, tile_counts):
    occ_total = amplitudes.shape[0]
    occ_row = occ_total // N_ROW
    slot_count = amplitudes.shape[2]
    tile_width = TILE
    live_slots = (jnp.arange(slot_count, dtype=jnp.int32)[None, :] < tile_counts[:, None]).astype(jnp.float32)

    def one_row(orbital):
        grid_group = (orbital // occ_row).astype(jnp.int32)
        tiles_b = lax.dynamic_index_in_dim(pair_lists, grid_group, 0, keepdims=False)[:, 1]
        chosen = jnp.take(integrals, tiles_b, axis=2).astype(jnp.float32)
        chosen = chosen.reshape(occ_total, occ_total, slot_count, tile_width, tile_width)
        amp_row = lax.dynamic_index_in_dim(amplitudes, orbital, 0, keepdims=False).astype(jnp.float32)
        amp_row = amp_row.reshape(occ_total, slot_count, tile_width, tile_width)
        row_out = jnp.einsum('ksac,kjscb->jsab', amp_row, chosen)
        keep_slots = lax.dynamic_index_in_dim(live_slots, grid_group, 0, keepdims=False)
        row_out = row_out * keep_slots[None, :, None, None]
        return row_out.reshape(occ_total, slot_count, tile_width * tile_width).astype(jnp.bfloat16)

    cycle = lax.map(one_row, jnp.arange(occ_total, dtype=jnp.int32))
    groups = jnp.arange(occ_total, dtype=jnp.int32) // occ_row
    tile_first = pair_lists[:, :, 0]
    tile_second = pair_lists[:, :, 1]
    pair_match = ((tile_first[:, None, :, None] == tile_second[None, :, None, :])
                  & (tile_second[:, None, :, None] == tile_first[None, :, None, :])).astype(jnp.float32)
    pair_match = pair_match[groups][:, groups]
    mirrored = jnp.swapaxes(cycle, 0, 1).astype(jnp.float32)
    mirrored = mirrored.reshape(occ_total, occ_total, slot_count, tile_width, tile_width)
    crossed = jnp.einsum('ijst,ijtba->ijsab', pair_match, mirrored)
    own_part = cycle.astype(jnp.float32).reshape(occ_total, occ_total, slot_count, tile_width, tile_width)
    keep_all = live_slots[groups]
    symmetric = (own_part + crossed) * keep_all[:, None, :, None, None]
    return symmetric.reshape(occ_total, occ_total, slot_count, tile_width * tile_width)
```

```python
import jax
import jax.numpy as jnp
from jax import lax
from jax.sharding import PartitionSpec as P

TILE = 64


def mirror_pairs(row_devices, col_devices, step):
    ratio = col_devices // row_devices
    pairs = []
    for row in range(row_devices):
        for col in range(col_devices):
            part = (col % ratio + step) % ratio
            pairs.append((row * col_devices + col, (col // ratio) * col_devices + row * ratio + part))
    return pairs


def on_device(amplitudes, integrals, pair_lists, tile_counts):
    occ_row, occ_col, slot_count, square = amplitudes.shape
    tile_width = TILE
    row_devices = lax.axis_size("row")
    col_devices = lax.axis_size("col")
    col_ratio = col_devices // row_devices
    my_row = lax.axis_index("row")
    my_col = lax.axis_index("col")
    partner_row = my_col // col_ratio
    tile_first = pair_lists[:, :, 0]
    tile_second = pair_lists[:, :, 1]
    packed = jnp.take(integrals, tile_second.reshape(-1), axis=2)
    packed = packed.reshape(occ_row, occ_col, row_devices, slot_count, square)
    received = lax.all_to_all(packed, "row", split_axis=2, concat_axis=0, tiled=True)
    received = received.reshape(occ_row * row_devices, occ_col, slot_count, square)
    piece = lax.all_gather(amplitudes, "col", axis=1, tiled=True)
    piece_count = piece.shape[1]
    left_tiles = piece.reshape(occ_row, piece_count, slot_count, tile_width, tile_width)
    right_tiles = received.reshape(piece_count, occ_col, slot_count, tile_width, tile_width)
    cycle_sum = jnp.einsum(
        "iksac,kjscb->ijsab", left_tiles, right_tiles, preferred_element_type=jnp.float32
    )
    my_count = lax.dynamic_index_in_dim(tile_counts, my_row, 0, keepdims=False)
    live_slots = (jnp.arange(slot_count, dtype=jnp.int32) < my_count).astype(jnp.float32)
    cycle_value = (cycle_sum * live_slots[None, None, :, None, None]).astype(jnp.bfloat16)
    cycle = cycle_value.reshape(occ_row, occ_col, slot_count, square)
    halves = cycle.reshape(col_ratio, occ_col, occ_col, slot_count, square)
    col_part = lax.rem(my_col, col_ratio)
    arrived = []
    for step in range(col_ratio):
        part = lax.rem(col_part + step, col_ratio)
        block = lax.dynamic_index_in_dim(halves, part, 0, keepdims=False)
        arrived.append(lax.ppermute(block, ("row", "col"), mirror_pairs(row_devices, col_devices, step)))
    arrived = jnp.stack(arrived)
    order = lax.rem(col_part - jnp.arange(col_ratio) + col_ratio, col_ratio)
    arrived = jnp.take(arrived, order, axis=0)
    mirror_block = jnp.moveaxis(arrived, 0, 1).reshape(occ_col, occ_row, slot_count, square)
    mirror_block = mirror_block.reshape(occ_col, occ_row, slot_count, tile_width, tile_width)
    mine_first = lax.dynamic_index_in_dim(tile_first, my_row, 0, keepdims=False)
    mine_second = lax.dynamic_index_in_dim(tile_second, my_row, 0, keepdims=False)
    their_first = lax.dynamic_index_in_dim(tile_first, partner_row, 0, keepdims=False)
    their_second = lax.dynamic_index_in_dim(tile_second, partner_row, 0, keepdims=False)
    pair_match = (
        (mine_first[:, None] == their_second[None, :])
        & (mine_second[:, None] == their_first[None, :])
    ).astype(jnp.bfloat16)
    crossed = jnp.einsum(
        "st,jitba->ijsab", pair_match, mirror_block, preferred_element_type=jnp.float32
    )
    own_part = cycle_value.astype(jnp.float32)
    symmetric = (own_part + crossed) * live_slots[None, None, :, None, None]
    return symmetric.reshape(occ_row, occ_col, slot_count, square)


def solution(mesh):
    return jax.shard_map(
        on_device,
        mesh=mesh,
        in_specs=(P("row", "col", None, None), P("row", "col", None, None), P(), P()),
        out_specs=P("row", "col", None, None),
        check_vma=False,
    )
```

```python
import functools

import jax
import jax.numpy as jnp
from jax import lax
from jax.experimental import pallas as pl
from jax.experimental.pallas import tpu as pltpu
from jax.sharding import PartitionSpec as P

TILE = 64
LANES = 128
CHUNKS = 3
VMEM = pl.BlockSpec(memory_space=pltpu.VMEM)
SMEM = pl.BlockSpec(memory_space=pltpu.SMEM)
ANY = pl.BlockSpec(memory_space=pl.ANY)
PARAMS = pltpu.CompilerParams(vmem_limit_bytes=48 * 1024 * 1024)


def rows_of(x):
    outer, pair, slots, square = x.shape
    x = jnp.transpose(x, (0, 2, 1, 3)).reshape(outer, slots, pair, square // LANES, LANES)
    return jnp.transpose(x, (0, 1, 3, 2, 4)).reshape(outer, slots, square // LANES * pair, LANES)


def tiles_of(x, pair):
    outer, slots, rows, lanes = x.shape
    x = x.reshape(outer, slots, rows // pair, pair, lanes)
    x = jnp.transpose(x, (0, 1, 3, 2, 4)).reshape(outer, slots, pair, rows // pair * lanes)
    return jnp.transpose(x, (0, 2, 1, 3))


def swap(x):
    count = x.shape[0]
    x = x.reshape(count // 8, 8, LANES)
    z = pltpu.roll(x, TILE, 2)
    after = pltpu.roll(z, 7, 1)
    before = pltpu.roll(z, 1, 1)
    odd = lax.broadcasted_iota(jnp.int32, x.shape, 1) % 2
    half = lax.broadcasted_iota(jnp.int32, x.shape, 2) // TILE
    out = jnp.where(odd == half, x, jnp.where(odd == 0, after, before))
    return out.reshape(count, LANES)


def pick_kernel(sizes, rows, list_ref, w_ref, *outs):
    my_row = lax.axis_index("row")
    depth = w_ref.shape[0]
    for shift in range(rows):
        row = lax.rem(my_row + shift, rows)
        base = 0
        for chunk, size in enumerate(sizes):
            out = outs[shift * len(sizes) + chunk]

            def one(s, _, base=base, out=out, row=row):
                tile = list_ref[row, 1, base + s]
                x = w_ref[:, tile].reshape(depth * TILE, LANES).astype(jnp.float32)
                out[s] = swap(x).astype(jnp.bfloat16)
                return 0

            lax.fori_loop(0, size, one, 0)
            base += size


def left_kernel(a_ref, out):
    depth, slots = a_ref.shape[:2]

    def one(s, _):
        x = a_ref[:, s].reshape(depth * TILE, LANES).astype(jnp.float32)
        out[s] = swap(x).astype(jnp.bfloat16)
        return 0

    lax.fori_loop(0, slots, one, 0)


def cycle_kernel(rows, cols, ratio, base, size, *refs):
    count_ref = refs[0]
    lefts = refs[1 : 1 + cols]
    rights = refs[1 + cols : 1 + cols + rows]
    outs = refs[1 + cols + rows : 1 + cols + rows + ratio]
    held_left, held_right, total, sem = refs[1 + cols + rows + ratio :]
    my_row = lax.axis_index("row")
    my_col = lax.axis_index("col")
    copies = []
    for e, left in enumerate(lefts):
        copies.append(pltpu.make_async_copy(left.at[pl.ds(base, size)], held_left.at[my_col ^ e], sem.at[len(copies)]))
    for d, right in enumerate(rights):
        row = lax.rem(my_row - d + rows, rows)
        copies.append(pltpu.make_async_copy(right, held_right.at[row], sem.at[len(copies)]))
    for copy in copies:
        copy.start()
    for copy in copies:
        copy.wait()
    my_count = count_ref[my_row]
    half = total.shape[0] // ratio

    def one(s, _):
        acc = None
        for row in range(rows):
            left = jnp.concatenate([held_left[row * ratio + p, s] for p in range(ratio)], axis=1)
            part = jnp.dot(left, held_right[row, s], preferred_element_type=jnp.float32)
            acc = part if acc is None else acc + part
        live = (base + s < my_count).astype(jnp.float32)
        total[...] = acc * live
        for step in range(ratio):
            part = lax.rem(lax.rem(my_col, ratio) + step, ratio)
            outs[step][s] = total[pl.ds(pl.multiple_of(part * half, half), half), :].astype(jnp.bfloat16)
        return 0

    lax.fori_loop(0, size, one, 0)


def final_kernel(rows, cols, ratio, sizes, list_ref, count_ref, *refs):
    chunks = len(sizes)
    owns = refs[: chunks * ratio]
    theirs = refs[chunks * ratio : 2 * chunks * ratio]
    out_ref, held_own, held_their, sem = refs[2 * chunks * ratio :]
    my_row = lax.axis_index("row")
    my_col = lax.axis_index("col")
    slots = sum(sizes)
    core = lax.rem(my_col, ratio)
    partner = my_col // ratio
    copies = []
    for step in range(ratio):
        mine = lax.rem(core + step, ratio)
        other = lax.rem(core - step + ratio, ratio)
        base = 0
        for chunk, size in enumerate(sizes):
            at = chunk * ratio + step
            copies.append(pltpu.make_async_copy(owns[at], held_own.at[mine, pl.ds(base, size)], sem.at[len(copies)]))
            copies.append(pltpu.make_async_copy(theirs[at], held_their.at[other, pl.ds(base, size)], sem.at[len(copies)]))
            base += size
    for copy in copies:
        copy.start()
    for copy in copies:
        copy.wait()
    my_count = count_ref[my_row]
    depth = out_ref.shape[0]

    def one(s, _):
        first = list_ref[my_row, 0, s]
        second = list_ref[my_row, 1, s]
        found = jnp.int32(-1)
        for t in range(slots):
            hit = (list_ref[partner, 0, t] == second) & (list_ref[partner, 1, t] == first)
            found = jnp.where(hit, t, found)
        live = s < my_count
        own = jnp.concatenate([held_own[p, s] for p in range(ratio)], axis=0).astype(jnp.float32)

        @pl.when(live & (found >= 0))
        def _():
            t = jnp.maximum(found, 0)
            mirror = jnp.concatenate([held_their[p, t].astype(jnp.float32).T for p in range(ratio)], axis=0)
            out_ref[:, s] = swap(own + mirror).reshape(depth, TILE, LANES)

        @pl.when(jnp.logical_not(live & (found >= 0)))
        def _():
            out_ref[:, s] = swap(own).reshape(depth, TILE, LANES)

        return 0

    lax.fori_loop(0, slots, one, 0)


def mirror_pairs(rows, cols, step):
    ratio = cols // rows
    pairs = []
    for row in range(rows):
        for col in range(cols):
            part = (col % ratio + step) % ratio
            pairs.append((row * cols + col, (col // ratio) * cols + row * ratio + part))
    return pairs


def on_device(amplitudes, integrals, pair_lists, tile_counts):
    rows = lax.axis_size("row")
    cols = lax.axis_size("col")
    ratio = cols // rows
    occ_row, occ_col, slots, square = amplitudes.shape
    assert occ_col * TILE == LANES and occ_row == ratio * occ_col
    sizes = [slots // CHUNKS] * CHUNKS
    tall = occ_row * TILE
    wide = occ_col * TILE
    lists = jnp.transpose(pair_lists, (0, 2, 1))
    bf16 = jnp.bfloat16

    picked = pl.pallas_call(
        functools.partial(pick_kernel, sizes, rows),
        out_shape=[jax.ShapeDtypeStruct((n, tall, wide), bf16) for _ in range(rows) for n in sizes],
        in_specs=[SMEM, VMEM],
        out_specs=[VMEM] * (rows * len(sizes)),
        compiler_params=PARAMS,
        name="pick",
    )(lists, rows_of(integrals))
    mine = pl.pallas_call(
        left_kernel,
        out_shape=jax.ShapeDtypeStruct((slots, tall, wide), bf16),
        in_specs=[VMEM],
        out_specs=VMEM,
        compiler_params=PARAMS,
        name="left",
    )(rows_of(amplitudes))

    rights = []
    for chunk in range(len(sizes)):
        got = [picked[chunk]]
        for shift in range(1, rows):
            pairs = [(r, (r + shift) % rows) for r in range(rows)]
            got.append(lax.ppermute(picked[shift * len(sizes) + chunk], "row", pairs))
        rights.append(got)

    lefts = [mine]
    for e in range(1, cols):
        if e % 2:
            lefts.append(lax.ppermute(lefts[e - 1], "col", [(c, c ^ 1) for c in range(cols)]))
        else:
            lefts.append(lax.ppermute(mine, "col", [(c, c ^ e) for c in range(cols)]))

    owns, theirs = [], []
    base = 0
    for chunk, size in enumerate(sizes):
        sent = pl.pallas_call(
            functools.partial(cycle_kernel, rows, cols, ratio, base, size),
            out_shape=[jax.ShapeDtypeStruct((size, tall // ratio, wide), bf16)] * ratio,
            in_specs=[SMEM] + [ANY] * (cols + rows),
            out_specs=[VMEM] * ratio,
            scratch_shapes=[
                pltpu.VMEM((cols, size, tall, wide), bf16),
                pltpu.VMEM((rows, size, tall, wide), bf16),
                pltpu.VMEM((tall, wide), jnp.float32),
                pltpu.SemaphoreType.DMA((cols + rows,)),
            ],
            compiler_params=PARAMS,
            name="cycle",
        )(tile_counts, *lefts, *rights[chunk])
        owns += sent
        for step in range(ratio):
            theirs.append(lax.ppermute(sent[step], ("row", "col"), mirror_pairs(rows, cols, step)))
        base += size

    out = pl.pallas_call(
        functools.partial(final_kernel, rows, cols, ratio, sizes),
        out_shape=jax.ShapeDtypeStruct((occ_row, slots, square // LANES * occ_col, LANES), jnp.float32),
        in_specs=[SMEM, SMEM] + [ANY] * (2 * len(sizes) * ratio),
        out_specs=VMEM,
        scratch_shapes=[
            pltpu.VMEM((ratio, slots, tall // ratio, wide), bf16),
            pltpu.VMEM((ratio, slots, tall // ratio, wide), bf16),
            pltpu.SemaphoreType.DMA((2 * len(sizes) * ratio,)),
        ],
        compiler_params=PARAMS,
        name="final",
    )(lists, tile_counts, *owns, *theirs)
    return tiles_of(out, occ_col)


def solution(mesh):
    return jax.shard_map(
        on_device,
        mesh=mesh,
        in_specs=(P("row", "col", None, None), P("row", "col", None, None), P(), P()),
        out_specs=P("row", "col", None, None),
        check_vma=False,
    )
```

```python
import functools

import jax
import jax.numpy as jnp
from jax import lax
from jax.experimental import pallas as pl
from jax.experimental.pallas import tpu as pltpu
from jax.sharding import PartitionSpec as P


TILE = 64
LANES = 128
CHUNKS = 3
VMEM = pl.BlockSpec(memory_space=pltpu.VMEM)
SMEM = pl.BlockSpec(memory_space=pltpu.SMEM)
ANY = pl.BlockSpec(memory_space=pl.ANY)
PARAMS = pltpu.CompilerParams(vmem_limit_bytes=48 * 1024 * 1024)


def rows_of(x):
    outer, pair, slots, square = x.shape
    x = jnp.transpose(x, (0, 2, 1, 3)).reshape(outer, slots, pair, square // LANES, LANES)
    return jnp.transpose(x, (0, 1, 3, 2, 4)).reshape(outer, slots, square // LANES * pair, LANES)


def tiles_of(x, pair):
    outer, slots, rows, lanes = x.shape
    x = x.reshape(outer, slots, rows // pair, pair, lanes)
    x = jnp.transpose(x, (0, 1, 3, 2, 4)).reshape(outer, slots, pair, rows // pair * lanes)
    return jnp.transpose(x, (0, 2, 1, 3))


def swap(x):
    count = x.shape[0]
    x = x.reshape(count // 8, 8, LANES)
    z = pltpu.roll(x, TILE, 2)
    after = pltpu.roll(z, 7, 1)
    before = pltpu.roll(z, 1, 1)
    odd = lax.broadcasted_iota(jnp.int32, x.shape, 1) % 2
    half = lax.broadcasted_iota(jnp.int32, x.shape, 2) // TILE
    out = jnp.where(odd == half, x, jnp.where(odd == 0, after, before))
    return out.reshape(count, LANES)


def pick_kernel(base, size, rows, list_ref, w_ref, *outs):
    my_row = lax.axis_index("row")
    depth = w_ref.shape[0]
    for shift in range(rows):
        row = lax.rem(my_row + shift, rows)
        out = outs[shift]

        def one(s, _, out=out, row=row):
            tile = list_ref[row, 1, base + s]
            x = w_ref[:, tile].reshape(depth * TILE, LANES).astype(jnp.float32)
            out[s] = swap(x).astype(jnp.bfloat16)
            return 0

        lax.fori_loop(0, size, one, 0)


def left_kernel(a_ref, out):
    depth, slots = a_ref.shape[:2]

    def one(s, _):
        x = a_ref[:, s].reshape(depth * TILE, LANES).astype(jnp.float32)
        out[s] = swap(x).astype(jnp.bfloat16)
        return 0

    lax.fori_loop(0, slots, one, 0)


def cycle_kernel(rows, cols, ratio, base, size, *refs):
    count_ref = refs[0]
    lefts = refs[1 : 1 + cols]
    rights = refs[1 + cols : 1 + cols + rows]
    outs = refs[1 + cols + rows : -4]
    held_left, held_right, total, sem = refs[-4:]
    my_row = lax.axis_index("row")
    my_col = lax.axis_index("col")
    copies = []
    for e, left in enumerate(lefts):
        copies.append(pltpu.make_async_copy(left.at[pl.ds(base, size)], held_left.at[my_col ^ e], sem.at[len(copies)]))
    for d, right in enumerate(rights):
        row = lax.rem(my_row - d + rows, rows)
        copies.append(pltpu.make_async_copy(right, held_right.at[row], sem.at[len(copies)]))
    for copy in copies:
        copy.start()
    for copy in copies:
        copy.wait()
    my_count = count_ref[my_row]
    half = total.shape[0] // ratio

    def one(hop, s, _):
        at = s
        s = s + hop * (size // 2)
        acc = None
        for row in range(rows):
            left = jnp.concatenate([held_left[row * ratio + p, s] for p in range(ratio)], axis=1)
            part = jnp.dot(left, held_right[row, s], preferred_element_type=jnp.float32)
            acc = part if acc is None else acc + part
        live = (base + s < my_count).astype(jnp.float32)
        total[...] = acc * live
        for step in range(ratio):
            part = lax.rem(lax.rem(my_col, ratio) + step, ratio)
            outs[2 * step + hop][at] = total[pl.ds(pl.multiple_of(part * half, half), half), :].astype(jnp.bfloat16)
        return 0

    for hop in range(2):
        lax.fori_loop(0, size // 2, functools.partial(one, hop), 0)


def final_kernel(ratio, sizes, list_ref, count_ref, *refs):
    chunks = len(sizes)
    owns = refs[: 2 * chunks * ratio]
    theirs = refs[2 * chunks * ratio : 4 * chunks * ratio]
    out_ref, held_own, held_their, sem = refs[-4:]
    my_row = lax.axis_index("row")
    my_col = lax.axis_index("col")
    slots = sum(sizes)
    core = lax.rem(my_col, ratio)
    partner = my_col // ratio
    copies = []
    for step in range(ratio):
        mine = lax.rem(core + step, ratio)
        other = lax.rem(core - step + ratio, ratio)
        base = 0
        for chunk, size in enumerate(sizes):
            for hop in range(2):
                at = (chunk * ratio + step) * 2 + hop
                where = pl.ds(base, size // 2)
                copies.append(pltpu.make_async_copy(owns[at], held_own.at[mine, where], sem.at[len(copies)]))
                copies.append(pltpu.make_async_copy(theirs[at], held_their.at[other, where], sem.at[len(copies)]))
                base += size // 2
    for copy in copies:
        copy.start()
    for copy in copies:
        copy.wait()
    my_count = count_ref[my_row]
    depth = out_ref.shape[0]

    def one(s, _):
        first = list_ref[my_row, 0, s]
        second = list_ref[my_row, 1, s]
        found = jnp.int32(-1)
        for t in range(slots):
            hit = (list_ref[partner, 0, t] == second) & (list_ref[partner, 1, t] == first)
            found = jnp.where(hit, t, found)
        live = s < my_count
        own = jnp.concatenate([held_own[p, s] for p in range(ratio)], axis=0).astype(jnp.float32)

        @pl.when(live & (found >= 0))
        def _():
            t = jnp.maximum(found, 0)
            mirror = jnp.concatenate([held_their[p, t].astype(jnp.float32).T for p in range(ratio)], axis=0)
            out_ref[:, s] = swap(own + mirror).reshape(depth, TILE, LANES)

        @pl.when(jnp.logical_not(live & (found >= 0)))
        def _():
            out_ref[:, s] = swap(own).reshape(depth, TILE, LANES)

        return 0

    lax.fori_loop(0, slots, one, 0)


def mirror_pairs(rows, cols, step, hop):
    ratio = cols // rows
    pairs = []
    for row in range(rows):
        for col in range(cols):
            part = (col % ratio + step) % ratio
            held = col ^ (hop * (cols // 2))
            pairs.append((row * cols + held, (col // ratio) * cols + row * ratio + part))
    return pairs


def on_device(amplitudes, integrals, pair_lists, tile_counts):
    rows = lax.axis_size("row")
    cols = lax.axis_size("col")
    ratio = cols // rows
    occ_row, occ_col, slots, square = amplitudes.shape
    assert occ_col * TILE == LANES and occ_row == ratio * occ_col
    sizes = [slots // CHUNKS] * CHUNKS
    tall = occ_row * TILE
    wide = occ_col * TILE
    lists = jnp.transpose(pair_lists, (0, 2, 1))
    bf16 = jnp.bfloat16

    table = rows_of(integrals)

    rights = []
    base = 0
    for size in sizes:
        picked = pl.pallas_call(
            functools.partial(pick_kernel, base, size, rows),
            out_shape=[jax.ShapeDtypeStruct((size, tall, wide), bf16)] * rows,
            in_specs=[SMEM, VMEM],
            out_specs=[VMEM] * rows,
            compiler_params=PARAMS,
            name="pick",
        )(lists, table)
        got = [picked[0]]
        for shift in range(1, rows):
            pairs = [(r, (r + shift) % rows) for r in range(rows)]
            got.append(lax.ppermute(picked[shift], "row", pairs))
        rights.append(got)
        base += size

    mine = pl.pallas_call(
        left_kernel,
        out_shape=jax.ShapeDtypeStruct((slots, tall, wide), bf16),
        in_specs=[VMEM],
        out_specs=VMEM,
        compiler_params=PARAMS,
        name="left",
    )(rows_of(amplitudes))
    lefts = [mine]
    for e in range(1, cols):
        if e % 2:
            lefts.append(lax.ppermute(lefts[e - 1], "col", [(c, c ^ 1) for c in range(cols)]))
        else:
            lefts.append(lax.ppermute(mine, "col", [(c, c ^ e) for c in range(cols)]))

    owns, theirs = [], []
    base = 0
    for chunk, size in enumerate(sizes):
        sent = pl.pallas_call(
            functools.partial(cycle_kernel, rows, cols, ratio, base, size),
            out_shape=[jax.ShapeDtypeStruct((size // 2, tall // ratio, wide), bf16)] * (2 * ratio),
            in_specs=[SMEM] + [ANY] * (cols + rows),
            out_specs=[VMEM] * (2 * ratio),
            scratch_shapes=[
                pltpu.VMEM((cols, size, tall, wide), bf16),
                pltpu.VMEM((rows, size, tall, wide), bf16),
                pltpu.VMEM((tall, wide), jnp.float32),
                pltpu.SemaphoreType.DMA((cols + rows,)),
            ],
            compiler_params=PARAMS,
            name="cycle",
        )(tile_counts, *lefts, *rights[chunk])
        owns += sent
        for step in range(ratio):
            for hop in range(2):
                block = sent[2 * step + hop]
                if hop:
                    block = lax.ppermute(block, "col", [(c, c ^ (cols // 2)) for c in range(cols)])
                theirs.append(lax.ppermute(block, ("row", "col"), mirror_pairs(rows, cols, step, hop)))
        base += size

    out = pl.pallas_call(
        functools.partial(final_kernel, ratio, sizes),
        out_shape=jax.ShapeDtypeStruct((occ_row, slots, square // LANES * occ_col, LANES), jnp.float32),
        in_specs=[SMEM, SMEM] + [ANY] * (4 * len(sizes) * ratio),
        out_specs=VMEM,
        scratch_shapes=[
            pltpu.VMEM((ratio, slots, tall // ratio, wide), bf16),
            pltpu.VMEM((ratio, slots, tall // ratio, wide), bf16),
            pltpu.SemaphoreType.DMA((4 * len(sizes) * ratio,)),
        ],
        compiler_params=PARAMS,
        name="final",
    )(lists, tile_counts, *owns, *theirs)
    return tiles_of(out, occ_col)


def solution(mesh):
    return jax.shard_map(
        on_device,
        mesh=mesh,
        in_specs=(P("row", "col", None, None), P("row", "col", None, None), P(), P()),
        out_specs=P("row", "col", None, None),
        check_vma=False,
    )
```

```python
import functools

import jax
import jax.numpy as jnp
from jax import lax
from jax.experimental import pallas as pl
from jax.experimental.pallas import tpu as pltpu
from jax.sharding import PartitionSpec as P


TILE = 64
LANES = 128
SPLIT = (5, 5, 2)
VMEM = pl.BlockSpec(memory_space=pltpu.VMEM)
SMEM = pl.BlockSpec(memory_space=pltpu.SMEM)
HBM = pl.BlockSpec(memory_space=pltpu.HBM)
PARAMS = pltpu.CompilerParams(vmem_limit_bytes=16 * 1024 * 1024)


def rows_of(x):
    outer, pair, slots, square = x.shape
    x = jnp.transpose(x, (0, 2, 1, 3)).reshape(outer, slots, pair, square // LANES, LANES)
    return jnp.transpose(x, (0, 1, 3, 2, 4)).reshape(outer, slots, square // LANES * pair, LANES)


def tiles_of(x, pair):
    outer, slots, rows, lanes = x.shape
    x = x.reshape(outer, slots, rows // pair, pair, lanes)
    x = jnp.transpose(x, (0, 1, 3, 2, 4)).reshape(outer, slots, pair, rows // pair * lanes)
    return jnp.transpose(x, (0, 2, 1, 3))


def swap(x):
    count = x.shape[0]
    x = x.reshape(count // 8, 8, LANES)
    z = pltpu.roll(x, TILE, 2)
    after = pltpu.roll(z, 7, 1)
    before = pltpu.roll(z, 1, 1)
    odd = lax.broadcasted_iota(jnp.int32, x.shape, 1) % 2
    half = lax.broadcasted_iota(jnp.int32, x.shape, 2) // TILE
    out = jnp.where(odd == half, x, jnp.where(odd == 0, after, before))
    return out.reshape(count, LANES)


def pick_kernel(base, size, rows, list_ref, w_ref, *outs):
    my_row = lax.axis_index("row")
    depth = w_ref.shape[0]
    for shift in range(rows):
        row = lax.rem(my_row + shift, rows)
        out = outs[shift]

        def one(s, _, out=out, row=row):
            tile = list_ref[row, 1, base + s]
            x = w_ref[:, tile].reshape(depth * TILE, LANES).astype(jnp.float32)
            out[s] = swap(x).astype(jnp.bfloat16)
            return 0

        lax.fori_loop(0, size, one, 0)


def left_kernel(a_ref, out):
    depth, slots = a_ref.shape[:2]

    def one(s, _):
        x = a_ref[:, s].reshape(depth * TILE, LANES).astype(jnp.float32)
        out[s] = swap(x).astype(jnp.bfloat16)
        return 0

    lax.fori_loop(0, slots, one, 0)


def cycle_kernel(rows, cols, ratio, base, size, *refs):
    count_ref = refs[0]
    lefts = refs[1 : 1 + cols]
    rights = refs[1 + cols : 1 + cols + rows]
    outs = refs[1 + cols + rows : -2]
    held, total = refs[-2:]
    my_row = lax.axis_index("row")
    my_col = lax.axis_index("col")
    core = lax.rem(my_col, ratio)
    half = total.shape[0] // ratio
    for d, right in enumerate(rights):
        row = lax.rem(my_row - d + rows, rows)
        for p in range(ratio):
            held[row, p] = right[:, pl.ds(pl.multiple_of((p ^ core) * half, half), half), :]
    my_count = count_ref[my_row]

    def one(s, _):
        acc = None
        for chip in range(rows):
            row = (my_col // ratio) ^ chip
            left = jnp.concatenate([lefts[chip * ratio + p][base + s] for p in range(ratio)], axis=1)
            right = jnp.concatenate([held[row, p, s] for p in range(ratio)], axis=0)
            part = jnp.dot(left, right, preferred_element_type=jnp.float32)
            acc = part if acc is None else acc + part
        live = (base + s < my_count).astype(jnp.float32)
        total[...] = acc * live
        for step in range(ratio):
            part = core ^ step
            outs[step][s] = total[pl.ds(pl.multiple_of(part * half, half), half), :].astype(jnp.bfloat16)
        return 0

    lax.fori_loop(0, size, one, 0)


def collect(refs, held, sizes, ratio, core):
    base = 0
    for chunk, size in enumerate(sizes):
        for step in range(ratio):
            held[core ^ step, base : base + size] = refs[chunk * ratio + step][...]
        base += size


def summed(held_own, s, held_their, t, ratio):
    own = jnp.concatenate([held_own[p, s] for p in range(ratio)], axis=0).astype(jnp.float32)
    if t is None:
        return own
    return own + jnp.concatenate([held_their[p, t].astype(jnp.float32).T for p in range(ratio)], axis=0)


def final_kernel(ratio, sizes, list_ref, count_ref, *refs):
    slots = sum(sizes)
    early = slots - sizes[-1]
    owns = refs[: len(sizes) * ratio]
    theirs = refs[len(sizes) * ratio : -3]
    out_ref, held_own, held_their = refs[-3:]
    my_row = lax.axis_index("row")
    my_col = lax.axis_index("col")
    core = lax.rem(my_col, ratio)
    partner = my_col // ratio
    collect(owns, held_own, sizes, ratio, core)
    collect(theirs, held_their, sizes[:-1], ratio, core)
    my_count = count_ref[my_row]
    depth = out_ref.shape[0]

    def one(s, _):
        first = list_ref[my_row, 0, s]
        second = list_ref[my_row, 1, s]
        found = jnp.int32(-1)
        for t in range(early):
            hit = (list_ref[partner, 0, t] == second) & (list_ref[partner, 1, t] == first)
            found = jnp.where(hit, t, found)
        use = (s < my_count) & (found >= 0)

        @pl.when(use)
        def _():
            x = summed(held_own, s, held_their, jnp.maximum(found, 0), ratio)
            out_ref[:, s] = swap(x).reshape(depth, TILE, LANES)

        @pl.when(jnp.logical_not(use))
        def _():
            x = summed(held_own, s, None, None, ratio)
            out_ref[:, s] = swap(x).reshape(depth, TILE, LANES)

        return 0

    lax.fori_loop(0, slots, one, 0)


def patch_kernel(ratio, sizes, list_ref, count_ref, *refs):
    slots = sum(sizes)
    early = slots - sizes[-1]
    owns = refs[: len(sizes) * ratio]
    theirs = refs[len(sizes) * ratio : -6]
    _, out_ref, held_own, held_their, built, sem = refs[-6:]
    my_row = lax.axis_index("row")
    my_col = lax.axis_index("col")
    core = lax.rem(my_col, ratio)
    partner = my_col // ratio
    collect(owns, held_own, sizes, ratio, core)
    collect(theirs, held_their, sizes[-1:], ratio, core)
    my_count = count_ref[my_row]
    depth = out_ref.shape[0]
    uses, copies = [], []
    for t in range(sizes[-1]):
        first = list_ref[partner, 0, early + t]
        second = list_ref[partner, 1, early + t]
        found = jnp.int32(-1)
        for s in range(slots):
            hit = (list_ref[my_row, 0, s] == second) & (list_ref[my_row, 1, s] == first)
            found = jnp.where(hit, s, found)
        uses.append((found < my_count) & (found >= 0))
        s = jnp.maximum(found, 0)
        copies.append(pltpu.make_async_copy(built.at[t], out_ref.at[:, s], sem.at[t]))

        @pl.when(uses[-1])
        def _(s=s, t=t):
            built[t] = swap(summed(held_own, s, held_their, t, ratio)).reshape(depth, TILE, LANES)
            copies[t].start()

    for use, copy in zip(uses, copies):
        pl.when(use)(copy.wait)


def mirror_pairs(rows, cols, step, hop):
    ratio = cols // rows
    pairs = []
    for row in range(rows):
        for col in range(cols):
            part = (col % ratio + step) % ratio
            held = col ^ (hop * (cols // 2))
            pairs.append((row * cols + held, (col // ratio) * cols + row * ratio + part))
    return pairs


def on_device(amplitudes, integrals, pair_lists, tile_counts):
    rows = lax.axis_size("row")
    cols = lax.axis_size("col")
    ratio = cols // rows
    occ_row, occ_col, slots, square = amplitudes.shape
    assert occ_col * TILE == LANES and occ_row == ratio * occ_col
    assert ratio == 2 and cols % 2 == 0 and cols & (cols - 1) == 0
    sizes = SPLIT if sum(SPLIT) == slots else (slots - 1, 1)
    tall = occ_row * TILE
    wide = occ_col * TILE
    lists = jnp.transpose(pair_lists, (0, 2, 1))
    bf16 = jnp.bfloat16

    table = rows_of(integrals)

    rights = []
    base = 0
    for size in sizes:
        picked = pl.pallas_call(
            functools.partial(pick_kernel, base, size, rows),
            out_shape=[jax.ShapeDtypeStruct((size, tall, wide), bf16)] * rows,
            in_specs=[SMEM, VMEM],
            out_specs=[VMEM] * rows,
            compiler_params=PARAMS,
            name="pick",
        )(lists, table)
        got = [picked[0]]
        for shift in range(1, rows):
            pairs = [(r, (r + shift) % rows) for r in range(rows)]
            got.append(lax.ppermute(picked[shift], "row", pairs))
        rights.append(got)
        base += size

    mine = pl.pallas_call(
        left_kernel,
        out_shape=jax.ShapeDtypeStruct((slots, tall, wide), bf16),
        in_specs=[VMEM],
        out_specs=VMEM,
        compiler_params=PARAMS,
        name="left",
    )(rows_of(amplitudes))
    lefts = [mine]
    for e in range(1, cols):
        if e % 2:
            lefts.append(lax.ppermute(lefts[e - 1], "col", [(c, c ^ 1) for c in range(cols)]))
        else:
            lefts.append(lax.ppermute(mine, "col", [(c, c ^ e) for c in range(cols)]))

    owns, theirs = [], []
    base = 0
    for chunk, size in enumerate(sizes):
        sent = pl.pallas_call(
            functools.partial(cycle_kernel, rows, cols, ratio, base, size),
            out_shape=[jax.ShapeDtypeStruct((size, tall // ratio, wide), bf16)] * ratio,
            in_specs=[SMEM] + [VMEM] * (cols + rows),
            out_specs=[VMEM] * ratio,
            scratch_shapes=[
                pltpu.VMEM((rows, ratio, size, tall // ratio, wide), bf16),
                pltpu.VMEM((tall, wide), jnp.float32),
            ],
            compiler_params=PARAMS,
            name="cycle",
        )(tile_counts, *lefts, *rights[chunk])
        owns += sent
        for step in range(ratio):
            block = sent[step]
            hop = step % 2
            if hop:
                block = lax.ppermute(block, "col", [(c, c ^ (cols // 2)) for c in range(cols)])
            theirs.append(lax.ppermute(block, ("row", "col"), mirror_pairs(rows, cols, step, hop)))
        base += size

    out_shape = jax.ShapeDtypeStruct((occ_row, slots, square // LANES * occ_col, LANES), jnp.float32)
    block = (tall // ratio, wide)
    split = ratio * (len(sizes) - 1)
    out = pl.pallas_call(
        functools.partial(final_kernel, ratio, sizes),
        out_shape=out_shape,
        in_specs=[SMEM, SMEM] + [VMEM] * (len(owns) + split),
        out_specs=VMEM,
        scratch_shapes=[
            pltpu.VMEM((ratio, slots) + block, bf16),
            pltpu.VMEM((ratio, slots - sizes[-1]) + block, bf16),
        ],
        compiler_params=PARAMS,
        name="final",
    )(lists, tile_counts, *owns, *theirs[:split])
    out = pl.pallas_call(
        functools.partial(patch_kernel, ratio, sizes),
        out_shape=out_shape,
        in_specs=[SMEM, SMEM] + [VMEM] * (len(owns) + ratio) + [HBM],
        out_specs=HBM,
        scratch_shapes=[
            pltpu.VMEM((ratio, slots) + block, bf16),
            pltpu.VMEM((ratio, sizes[-1]) + block, bf16),
            pltpu.VMEM((sizes[-1], occ_row, TILE, LANES), jnp.float32),
            pltpu.SemaphoreType.DMA((sizes[-1],)),
        ],
        input_output_aliases={2 + len(owns) + ratio: 0},
        compiler_params=PARAMS,
        name="patch",
    )(lists, tile_counts, *owns, *theirs[split:], out)
    return tiles_of(out, occ_col)


def solution(mesh):
    return jax.shard_map(
        on_device,
        mesh=mesh,
        in_specs=(P("row", "col", None, None), P("row", "col", None, None), P(), P()),
        out_specs=P("row", "col", None, None),
        check_vma=False,
    )
```

```python
import functools

import jax
import jax.numpy as jnp
from jax import lax
from jax.experimental import pallas as pl
from jax.experimental.pallas import tpu as pltpu
from jax.sharding import PartitionSpec as P


TILE = 64
LANES = 128
SPLIT = (5, 5, 2)
HOPPED = (True, True, False)
VMEM = pl.BlockSpec(memory_space=pltpu.VMEM)
SMEM = pl.BlockSpec(memory_space=pltpu.SMEM)
HBM = pl.BlockSpec(memory_space=pltpu.HBM)
PARAMS = pltpu.CompilerParams(vmem_limit_bytes=16 * 1024 * 1024)


def rows_of(x):
    outer, pair, slots, square = x.shape
    x = jnp.transpose(x, (0, 2, 1, 3)).reshape(outer, slots, pair, square // LANES, LANES)
    return jnp.transpose(x, (0, 1, 3, 2, 4)).reshape(outer, slots, square // LANES * pair, LANES)


def tiles_of(x, pair):
    outer, slots, rows, lanes = x.shape
    x = x.reshape(outer, slots, rows // pair, pair, lanes)
    x = jnp.transpose(x, (0, 1, 3, 2, 4)).reshape(outer, slots, pair, rows // pair * lanes)
    return jnp.transpose(x, (0, 2, 1, 3))


def swap(x):
    count = x.shape[0]
    x = x.reshape(count // 8, 8, LANES)
    z = pltpu.roll(x, TILE, 2)
    after = pltpu.roll(z, 7, 1)
    before = pltpu.roll(z, 1, 1)
    odd = lax.broadcasted_iota(jnp.int32, x.shape, 1) % 2
    half = lax.broadcasted_iota(jnp.int32, x.shape, 2) // TILE
    out = jnp.where(odd == half, x, jnp.where(odd == 0, after, before))
    return out.reshape(count, LANES)


def pick_kernel(base, size, rows, list_ref, w_ref, *outs):
    my_row = lax.axis_index("row")
    depth = w_ref.shape[0]
    for shift in range(rows):
        row = lax.rem(my_row + shift, rows)
        out = outs[shift]

        def one(s, _, out=out, row=row):
            tile = list_ref[row, 1, base + s]
            x = w_ref[:, tile].reshape(depth * TILE, LANES).astype(jnp.float32)
            out[s] = swap(x).astype(jnp.bfloat16)
            return 0

        lax.fori_loop(0, size, one, 0)


def left_kernel(a_ref, *outs):
    depth = a_ref.shape[0]
    base = 0
    for out in outs:

        def one(s, _, out=out, base=base):
            x = a_ref[:, base + s].reshape(depth * TILE, LANES).astype(jnp.float32)
            out[s] = swap(x).astype(jnp.bfloat16)
            return 0

        lax.fori_loop(0, out.shape[0], one, 0)
        base += out.shape[0]


def cycle_kernel(rows, cols, ratio, base, skip, size, *refs):
    count_ref = refs[0]
    lefts = refs[1 : 1 + cols]
    rights = refs[1 + cols : 1 + cols + rows]
    outs = refs[1 + cols + rows : -2]
    held, total = refs[-2:]
    my_row = lax.axis_index("row")
    my_col = lax.axis_index("col")
    core = lax.rem(my_col, ratio)
    half = total.shape[0] // ratio
    for d, right in enumerate(rights):
        row = lax.rem(my_row - d + rows, rows)
        for p in range(ratio):
            held[row, p] = right[:, pl.ds(pl.multiple_of((p ^ core) * half, half), half), :]
    my_count = count_ref[my_row]

    def one(s, _):
        acc = None
        for chip in range(rows):
            row = (my_col // ratio) ^ chip
            left = jnp.concatenate([lefts[chip * ratio + p][skip + s] for p in range(ratio)], axis=1)
            right = jnp.concatenate([held[row, p, s] for p in range(ratio)], axis=0)
            part = jnp.dot(left, right, preferred_element_type=jnp.float32)
            acc = part if acc is None else acc + part
        live = (base + s < my_count).astype(jnp.float32)
        total[...] = acc * live
        for step in range(ratio):
            part = core ^ step
            outs[step][s] = total[pl.ds(pl.multiple_of(part * half, half), half), :].astype(jnp.bfloat16)
        return 0

    lax.fori_loop(0, size, one, 0)


def collect(refs, held, sizes, ratio, core):
    base = 0
    for chunk, size in enumerate(sizes):
        for step in range(ratio):
            held[core ^ step, base : base + size] = refs[chunk * ratio + step][...]
        base += size


def summed(held_own, s, held_their, t, ratio):
    own = jnp.concatenate([held_own[p, s] for p in range(ratio)], axis=0).astype(jnp.float32)
    if t is None:
        return own
    return own + jnp.concatenate([held_their[p, t].astype(jnp.float32).T for p in range(ratio)], axis=0)


def final_kernel(ratio, sizes, list_ref, count_ref, *refs):
    slots = sum(sizes)
    early = sizes[0]
    owns = refs[: len(sizes) * ratio]
    theirs = refs[len(sizes) * ratio : -3]
    out_ref, held_own, held_their = refs[-3:]
    my_row = lax.axis_index("row")
    my_col = lax.axis_index("col")
    core = lax.rem(my_col, ratio)
    partner = my_col // ratio
    collect(owns, held_own, sizes, ratio, core)
    collect(theirs, held_their, sizes[:1], ratio, core)
    my_count = count_ref[my_row]
    depth = out_ref.shape[0]

    def one(s, _):
        first = list_ref[my_row, 0, s]
        second = list_ref[my_row, 1, s]
        found = jnp.int32(-1)
        for t in range(early):
            hit = (list_ref[partner, 0, t] == second) & (list_ref[partner, 1, t] == first)
            found = jnp.where(hit, t, found)
        use = (s < my_count) & (found >= 0)

        @pl.when(use)
        def _():
            x = summed(held_own, s, held_their, jnp.maximum(found, 0), ratio)
            out_ref[:, s] = swap(x).reshape(depth, TILE, LANES)

        @pl.when(jnp.logical_not(use))
        def _():
            x = summed(held_own, s, None, None, ratio)
            out_ref[:, s] = swap(x).reshape(depth, TILE, LANES)

        return 0

    lax.fori_loop(0, slots, one, 0)


def patch_kernel(ratio, sizes, list_ref, count_ref, *refs):
    slots = sum(sizes)
    early = sizes[0]
    owns = refs[: len(sizes) * ratio]
    theirs = refs[len(sizes) * ratio : -6]
    _, out_ref, held_own, held_their, built, sem = refs[-6:]
    my_row = lax.axis_index("row")
    my_col = lax.axis_index("col")
    core = lax.rem(my_col, ratio)
    partner = my_col // ratio
    collect(owns, held_own, sizes, ratio, core)
    collect(theirs, held_their, sizes[1:], ratio, core)
    my_count = count_ref[my_row]
    depth = out_ref.shape[0]
    uses, copies = [], []
    for t in range(slots - early):
        first = list_ref[partner, 0, early + t]
        second = list_ref[partner, 1, early + t]
        found = jnp.int32(-1)
        for s in range(slots):
            hit = (list_ref[my_row, 0, s] == second) & (list_ref[my_row, 1, s] == first)
            found = jnp.where(hit, s, found)
        uses.append((found < my_count) & (found >= 0))
        s = jnp.maximum(found, 0)
        copies.append(pltpu.make_async_copy(built.at[t], out_ref.at[:, s], sem.at[t]))

        @pl.when(uses[-1])
        def _(s=s, t=t):
            built[t] = swap(summed(held_own, s, held_their, t, ratio)).reshape(depth, TILE, LANES)
            copies[t].start()

    for use, copy in zip(uses, copies):
        pl.when(use)(copy.wait)


def mirror_pairs(rows, cols, step, hop):
    ratio = cols // rows
    pairs = []
    for row in range(rows):
        for col in range(cols):
            part = (col % ratio + step) % ratio
            held = col ^ (hop * (cols // 2))
            pairs.append((row * cols + held, (col // ratio) * cols + row * ratio + part))
    return pairs


def on_device(amplitudes, integrals, pair_lists, tile_counts):
    rows = lax.axis_size("row")
    cols = lax.axis_size("col")
    ratio = cols // rows
    occ_row, occ_col, slots, square = amplitudes.shape
    assert occ_col * TILE == LANES and occ_row == ratio * occ_col
    assert ratio == 2 and cols % 2 == 0 and cols & (cols - 1) == 0
    sizes = SPLIT if sum(SPLIT) == slots else (slots - 1, 1)
    tall = occ_row * TILE
    wide = occ_col * TILE
    lists = jnp.transpose(pair_lists, (0, 2, 1))
    bf16 = jnp.bfloat16

    table = rows_of(integrals)

    rights = []
    base = 0
    for size in sizes:
        picked = pl.pallas_call(
            functools.partial(pick_kernel, base, size, rows),
            out_shape=[jax.ShapeDtypeStruct((size, tall, wide), bf16)] * rows,
            in_specs=[SMEM, VMEM],
            out_specs=[VMEM] * rows,
            compiler_params=PARAMS,
            name="pick",
        )(lists, table)
        got = [picked[0]]
        for shift in range(1, rows):
            pairs = [(r, (r + shift) % rows) for r in range(rows)]
            got.append(lax.ppermute(picked[shift], "row", pairs))
        rights.append(got)
        base += size

    parts = (sizes[0], slots - sizes[0])
    mine = pl.pallas_call(
        left_kernel,
        out_shape=[jax.ShapeDtypeStruct((n, tall, wide), bf16) for n in parts],
        in_specs=[VMEM],
        out_specs=[VMEM] * 2,
        compiler_params=PARAMS,
        name="left",
    )(rows_of(amplitudes))
    lefts = []
    for part in range(2):
        got = [mine[part]]
        for e in range(1, cols):
            source = got[e - 1] if e % 2 else got[0]
            step = 1 if e % 2 else e
            got.append(lax.ppermute(source, "col", [(c, c ^ step) for c in range(cols)]))
        lefts.append(got)

    owns, theirs = [], []
    base = 0
    for chunk, size in enumerate(sizes):
        sent = pl.pallas_call(
            functools.partial(cycle_kernel, rows, cols, ratio, base, base if chunk == 0 else base - sizes[0], size),
            out_shape=[jax.ShapeDtypeStruct((size, tall // ratio, wide), bf16)] * ratio,
            in_specs=[SMEM] + [VMEM] * (cols + rows),
            out_specs=[VMEM] * ratio,
            scratch_shapes=[
                pltpu.VMEM((rows, ratio, size, tall // ratio, wide), bf16),
                pltpu.VMEM((tall, wide), jnp.float32),
            ],
            compiler_params=PARAMS,
            name="cycle",
        )(tile_counts, *lefts[min(chunk, 1)], *rights[chunk])
        owns += sent
        for step in range(ratio):
            block = sent[step]
            hop = step % 2 if HOPPED[chunk] else 0
            if hop:
                block = lax.ppermute(block, "col", [(c, c ^ (cols // 2)) for c in range(cols)])
            theirs.append(lax.ppermute(block, ("row", "col"), mirror_pairs(rows, cols, step, hop)))
        base += size

    out_shape = jax.ShapeDtypeStruct((occ_row, slots, square // LANES * occ_col, LANES), jnp.float32)
    block = (tall // ratio, wide)
    split = ratio
    late = slots - sizes[0]
    out = pl.pallas_call(
        functools.partial(final_kernel, ratio, sizes),
        out_shape=out_shape,
        in_specs=[SMEM, SMEM] + [VMEM] * (len(owns) + split),
        out_specs=VMEM,
        scratch_shapes=[
            pltpu.VMEM((ratio, slots) + block, bf16),
            pltpu.VMEM((ratio, sizes[0]) + block, bf16),
        ],
        compiler_params=PARAMS,
        name="final",
    )(lists, tile_counts, *owns, *theirs[:split])
    out = pl.pallas_call(
        functools.partial(patch_kernel, ratio, sizes),
        out_shape=out_shape,
        in_specs=[SMEM, SMEM] + [VMEM] * (len(owns) + len(theirs) - split) + [HBM],
        out_specs=HBM,
        scratch_shapes=[
            pltpu.VMEM((ratio, slots) + block, bf16),
            pltpu.VMEM((ratio, late) + block, bf16),
            pltpu.VMEM((late, occ_row, TILE, LANES), jnp.float32),
            pltpu.SemaphoreType.DMA((late,)),
        ],
        input_output_aliases={2 + len(owns) + len(theirs) - split: 0},
        compiler_params=PARAMS,
        name="patch",
    )(lists, tile_counts, *owns, *theirs[split:], out)
    return tiles_of(out, occ_col)


def solution(mesh):
    return jax.shard_map(
        on_device,
        mesh=mesh,
        in_specs=(P("row", "col", None, None), P("row", "col", None, None), P(), P()),
        out_specs=P("row", "col", None, None),
        check_vma=False,
    )
```

```python
import functools

import jax
import jax.numpy as jnp
from jax import lax
from jax.experimental import pallas as pl
from jax.experimental.pallas import tpu as pltpu
from jax.sharding import PartitionSpec as P


TILE = 64
LANES = 128
SPLIT = (5, 5, 2)
HOPPED = (True, True, True)
VMEM = pl.BlockSpec(memory_space=pltpu.VMEM)
SMEM = pl.BlockSpec(memory_space=pltpu.SMEM)
HBM = pl.BlockSpec(memory_space=pltpu.HBM)
PARAMS = pltpu.CompilerParams(vmem_limit_bytes=16 * 1024 * 1024)


def rows_of(x):
    outer, pair, slots, square = x.shape
    x = jnp.transpose(x, (0, 2, 1, 3)).reshape(outer, slots, pair, square // LANES, LANES)
    return jnp.transpose(x, (0, 1, 3, 2, 4)).reshape(outer, slots, square // LANES * pair, LANES)


def tiles_of(x, pair):
    outer, slots, rows, lanes = x.shape
    x = x.reshape(outer, slots, rows // pair, pair, lanes)
    x = jnp.transpose(x, (0, 1, 3, 2, 4)).reshape(outer, slots, pair, rows // pair * lanes)
    return jnp.transpose(x, (0, 2, 1, 3))


def swap(x):
    count = x.shape[0]
    x = x.reshape(count // 8, 8, LANES)
    odd = lax.broadcasted_iota(jnp.int32, x.shape, 1) % 2
    half = lax.broadcasted_iota(jnp.int32, x.shape, 2) // TILE
    other = jnp.where(odd == 0, pltpu.roll(x, 7, 1), pltpu.roll(x, 1, 1))
    out = jnp.where(odd == half, x, pltpu.roll(other, TILE, 2))
    return out.reshape(count, LANES)


def pick_kernel(base, size, rows, list_ref, w_ref, *outs):
    my_row = lax.axis_index("row")
    depth = w_ref.shape[0]
    for shift in range(rows):
        row = lax.rem(my_row + shift, rows)
        out = outs[shift]

        def one(s, _, out=out, row=row):
            tile = list_ref[row, 1, base + s]
            x = w_ref[:, tile].reshape(depth * TILE, LANES).astype(jnp.float32)
            out[s] = swap(x).astype(jnp.bfloat16)
            return 0

        lax.fori_loop(0, size, one, 0, unroll=True)


def left_kernel(a_ref, *outs):
    depth = a_ref.shape[0]
    base = 0
    for out in outs:

        def one(s, _, out=out, base=base):
            x = a_ref[:, base + s].reshape(depth * TILE, LANES).astype(jnp.float32)
            out[s] = swap(x).astype(jnp.bfloat16)
            return 0

        lax.fori_loop(0, out.shape[0], one, 0, unroll=True)
        base += out.shape[0]


def cycle_kernel(rows, cols, ratio, base, skip, size, *refs):
    count_ref = refs[0]
    lefts = refs[1 : 1 + cols]
    rights = refs[1 + cols : 1 + cols + rows]
    outs = refs[1 + cols + rows : -2]
    held, total = refs[-2:]
    my_row = lax.axis_index("row")
    my_col = lax.axis_index("col")
    core = lax.rem(my_col, ratio)
    half = total.shape[0] // ratio
    for d, right in enumerate(rights):
        row = lax.rem(my_row - d + rows, rows)
        for p in range(ratio):
            held[row, p] = right[:, pl.ds(pl.multiple_of((p ^ core) * half, half), half), :]
    my_count = count_ref[my_row]

    def one(s, _):
        acc = None
        for chip in range(rows):
            row = (my_col // ratio) ^ chip
            left = jnp.concatenate([lefts[chip * ratio + p][skip + s] for p in range(ratio)], axis=1)
            right = jnp.concatenate([held[row, p, s] for p in range(ratio)], axis=0)
            part = jnp.dot(left, right, preferred_element_type=jnp.float32)
            acc = part if acc is None else acc + part
        live = (base + s < my_count).astype(jnp.float32)
        total[...] = acc * live
        for step in range(ratio):
            part = core ^ step
            outs[step][s] = total[pl.ds(pl.multiple_of(part * half, half), half), :].astype(jnp.bfloat16)
        return 0

    lax.fori_loop(0, size, one, 0)


def collect(refs, held, sizes, ratio, core):
    base = 0
    for chunk, size in enumerate(sizes):
        for step in range(ratio):
            held[core ^ step, base : base + size] = refs[chunk * ratio + step][...]
        base += size


def summed(held_own, s, held_their, t, ratio):
    own = jnp.concatenate([held_own[p, s] for p in range(ratio)], axis=0).astype(jnp.float32)
    if t is None:
        return own
    return own + jnp.concatenate([held_their[p, t].astype(jnp.float32).T for p in range(ratio)], axis=0)


def final_kernel(ratio, sizes, list_ref, count_ref, *refs):
    slots = sum(sizes)
    early = sizes[0]
    owns = refs[: len(sizes) * ratio]
    theirs = refs[len(sizes) * ratio : -3]
    out_ref, held_own, held_their = refs[-3:]
    my_row = lax.axis_index("row")
    my_col = lax.axis_index("col")
    core = lax.rem(my_col, ratio)
    partner = my_col // ratio
    collect(owns, held_own, sizes, ratio, core)
    collect(theirs, held_their, sizes[:1], ratio, core)
    my_count = count_ref[my_row]
    depth = out_ref.shape[0]

    def one(s, _):
        first = list_ref[my_row, 0, s]
        second = list_ref[my_row, 1, s]
        found = jnp.int32(-1)
        for t in range(early):
            hit = (list_ref[partner, 0, t] == second) & (list_ref[partner, 1, t] == first)
            found = jnp.where(hit, t, found)
        use = (s < my_count) & (found >= 0)

        @pl.when(use)
        def _():
            x = summed(held_own, s, held_their, jnp.maximum(found, 0), ratio)
            out_ref[:, s] = swap(x).reshape(depth, TILE, LANES)

        @pl.when(jnp.logical_not(use))
        def _():
            x = summed(held_own, s, None, None, ratio)
            out_ref[:, s] = swap(x).reshape(depth, TILE, LANES)

        return 0

    lax.fori_loop(0, slots, one, 0)


def patch_kernel(ratio, sizes, list_ref, count_ref, *refs):
    slots = sum(sizes)
    early = sizes[0]
    owns = refs[: len(sizes) * ratio]
    theirs = refs[len(sizes) * ratio : -6]
    _, out_ref, held_own, held_their, built, sem = refs[-6:]
    my_row = lax.axis_index("row")
    my_col = lax.axis_index("col")
    core = lax.rem(my_col, ratio)
    partner = my_col // ratio
    collect(owns, held_own, sizes, ratio, core)
    collect(theirs, held_their, sizes[1:], ratio, core)
    my_count = count_ref[my_row]
    depth = out_ref.shape[0]
    uses, copies = [], []
    for t in range(slots - early):
        first = list_ref[partner, 0, early + t]
        second = list_ref[partner, 1, early + t]
        found = jnp.int32(-1)
        for s in range(slots):
            hit = (list_ref[my_row, 0, s] == second) & (list_ref[my_row, 1, s] == first)
            found = jnp.where(hit, s, found)
        uses.append((found < my_count) & (found >= 0))
        s = jnp.maximum(found, 0)
        copies.append(pltpu.make_async_copy(built.at[t], out_ref.at[:, s], sem.at[t]))

        @pl.when(uses[-1])
        def _(s=s, t=t):
            built[t] = swap(summed(held_own, s, held_their, t, ratio)).reshape(depth, TILE, LANES)
            copies[t].start()

    for use, copy in zip(uses, copies):
        pl.when(use)(copy.wait)


def mirror_pairs(rows, cols, step, hop):
    ratio = cols // rows
    pairs = []
    for row in range(rows):
        for col in range(cols):
            part = (col % ratio + step) % ratio
            held = col ^ (hop * (cols // 2))
            pairs.append((row * cols + held, (col // ratio) * cols + row * ratio + part))
    return pairs


def on_device(amplitudes, integrals, pair_lists, tile_counts):
    rows = lax.axis_size("row")
    cols = lax.axis_size("col")
    ratio = cols // rows
    occ_row, occ_col, slots, square = amplitudes.shape
    assert occ_col * TILE == LANES and occ_row == ratio * occ_col
    assert ratio == 2 and cols % 2 == 0 and cols & (cols - 1) == 0
    sizes = SPLIT if sum(SPLIT) == slots else (slots - 1, 1)
    tall = occ_row * TILE
    wide = occ_col * TILE
    lists = jnp.transpose(pair_lists, (0, 2, 1))
    bf16 = jnp.bfloat16

    table = rows_of(integrals)

    rights = []
    base = 0
    for size in sizes:
        picked = pl.pallas_call(
            functools.partial(pick_kernel, base, size, rows),
            out_shape=[jax.ShapeDtypeStruct((size, tall, wide), bf16)] * rows,
            in_specs=[SMEM, VMEM],
            out_specs=[VMEM] * rows,
            compiler_params=PARAMS,
            name="pick",
        )(lists, table)
        got = [picked[0]]
        for shift in range(1, rows):
            pairs = [(r, (r + shift) % rows) for r in range(rows)]
            got.append(lax.ppermute(picked[shift], "row", pairs))
        rights.append(got)
        base += size

    parts = (sizes[0], slots - sizes[0])
    mine = pl.pallas_call(
        left_kernel,
        out_shape=[jax.ShapeDtypeStruct((n, tall, wide), bf16) for n in parts],
        in_specs=[VMEM],
        out_specs=[VMEM] * 2,
        compiler_params=PARAMS,
        name="left",
    )(rows_of(amplitudes))
    lefts = []
    for part in range(2):
        got = [mine[part]]
        for e in range(1, cols):
            source = got[e - 1] if e % 2 else got[0]
            step = 1 if e % 2 else e
            got.append(lax.ppermute(source, "col", [(c, c ^ step) for c in range(cols)]))
        lefts.append(got)

    owns, theirs = [], []
    base = 0
    for chunk, size in enumerate(sizes):
        sent = pl.pallas_call(
            functools.partial(cycle_kernel, rows, cols, ratio, base, base if chunk == 0 else base - sizes[0], size),
            out_shape=[jax.ShapeDtypeStruct((size, tall // ratio, wide), bf16)] * ratio,
            in_specs=[SMEM] + [VMEM] * (cols + rows),
            out_specs=[VMEM] * ratio,
            scratch_shapes=[
                pltpu.VMEM((rows, ratio, size, tall // ratio, wide), bf16),
                pltpu.VMEM((tall, wide), jnp.float32),
            ],
            compiler_params=PARAMS,
            name="cycle",
        )(tile_counts, *lefts[min(chunk, 1)], *rights[chunk])
        owns += sent
        for step in range(ratio):
            block = sent[step]
            hop = step % 2 if HOPPED[chunk] else 0
            if hop:
                block = lax.ppermute(block, "col", [(c, c ^ (cols // 2)) for c in range(cols)])
            theirs.append(lax.ppermute(block, ("row", "col"), mirror_pairs(rows, cols, step, hop)))
        base += size

    out_shape = jax.ShapeDtypeStruct((occ_row, slots, square // LANES * occ_col, LANES), jnp.float32)
    block = (tall // ratio, wide)
    split = ratio
    late = slots - sizes[0]
    out = pl.pallas_call(
        functools.partial(final_kernel, ratio, sizes),
        out_shape=out_shape,
        in_specs=[SMEM, SMEM] + [VMEM] * (len(owns) + split),
        out_specs=VMEM,
        scratch_shapes=[
            pltpu.VMEM((ratio, slots) + block, bf16),
            pltpu.VMEM((ratio, sizes[0]) + block, bf16),
        ],
        compiler_params=PARAMS,
        name="final",
    )(lists, tile_counts, *owns, *theirs[:split])
    out = pl.pallas_call(
        functools.partial(patch_kernel, ratio, sizes),
        out_shape=out_shape,
        in_specs=[SMEM, SMEM] + [VMEM] * (len(owns) + len(theirs) - split) + [HBM],
        out_specs=HBM,
        scratch_shapes=[
            pltpu.VMEM((ratio, slots) + block, bf16),
            pltpu.VMEM((ratio, late) + block, bf16),
            pltpu.VMEM((late, occ_row, TILE, LANES), jnp.float32),
            pltpu.SemaphoreType.DMA((late,)),
        ],
        input_output_aliases={2 + len(owns) + len(theirs) - split: 0},
        compiler_params=PARAMS,
        name="patch",
    )(lists, tile_counts, *owns, *theirs[split:], out)
    return tiles_of(out, occ_col)


def solution(mesh):
    return jax.shard_map(
        on_device,
        mesh=mesh,
        in_specs=(P("row", "col", None, None), P("row", "col", None, None), P(), P()),
        out_specs=P("row", "col", None, None),
        check_vma=False,
    )
```

```python
import functools

import jax
import jax.numpy as jnp
from jax import lax
from jax.experimental import pallas as pl
from jax.experimental.pallas import tpu as pltpu
from jax.sharding import PartitionSpec as P


TILE = 64
LANES = 128
SPLIT = (6, 4, 2)
HOPS = ((1, 3), (0, 2), (0, 2))
VMEM = pl.BlockSpec(memory_space=pltpu.VMEM)
SMEM = pl.BlockSpec(memory_space=pltpu.SMEM)
HBM = pl.BlockSpec(memory_space=pltpu.HBM)
PARAMS = pltpu.CompilerParams(vmem_limit_bytes=16 * 1024 * 1024)


def rows_of(x):
    outer, pair, slots, square = x.shape
    x = jnp.transpose(x, (0, 2, 1, 3)).reshape(outer, slots, pair, square // LANES, LANES)
    return jnp.transpose(x, (0, 1, 3, 2, 4)).reshape(outer, slots, square // LANES * pair, LANES)


def tiles_of(x, pair):
    outer, slots, rows, lanes = x.shape
    x = x.reshape(outer, slots, rows // pair, pair, lanes)
    x = jnp.transpose(x, (0, 1, 3, 2, 4)).reshape(outer, slots, pair, rows // pair * lanes)
    return jnp.transpose(x, (0, 2, 1, 3))


def swap(x):
    count = x.shape[0]
    x = x.reshape(count // 8, 8, LANES)
    odd = lax.broadcasted_iota(jnp.int32, x.shape, 1) % 2
    half = lax.broadcasted_iota(jnp.int32, x.shape, 2) // TILE
    other = jnp.where(odd == 0, pltpu.roll(x, 7, 1), pltpu.roll(x, 1, 1))
    out = jnp.where(odd == half, x, pltpu.roll(other, TILE, 2))
    return out.reshape(count, LANES)


def pick_kernel(base, size, rows, list_ref, w_ref, *outs):
    my_row = lax.axis_index("row")
    depth = w_ref.shape[0]
    for shift in range(rows):
        row = my_row ^ shift
        out = outs[shift]

        def one(s, _, out=out, row=row):
            tile = list_ref[row, 1, base + s]
            x = w_ref[:, tile].reshape(depth * TILE, LANES).astype(jnp.float32)
            out[s] = swap(x).astype(jnp.bfloat16)
            return 0

        lax.fori_loop(0, size, one, 0, unroll=True)


def left_kernel(a_ref, *outs):
    depth = a_ref.shape[0]
    base = 0
    for out in outs:

        def one(s, _, out=out, base=base):
            x = a_ref[:, base + s].reshape(depth * TILE, LANES).astype(jnp.float32)
            out[s] = swap(x).astype(jnp.bfloat16)
            return 0

        lax.fori_loop(0, out.shape[0], one, 0, unroll=True)
        base += out.shape[0]


def cycle_kernel(rows, cols, ratio, base, skip, size, *refs):
    count_ref = refs[0]
    lefts = refs[1 : 1 + cols]
    rights = refs[1 + cols : 1 + cols + rows]
    outs = refs[1 + cols + rows : -2]
    held, total = refs[-2:]
    my_row = lax.axis_index("row")
    my_col = lax.axis_index("col")
    core = lax.rem(my_col, ratio)
    half = total.shape[0] // ratio
    for d, right in enumerate(rights):
        row = my_row ^ d
        for p in range(ratio):
            held[row, p] = right[:, pl.ds(pl.multiple_of((p ^ core) * half, half), half), :]
    my_count = count_ref[my_row]

    def one(s, _):
        acc = None
        for chip in range(rows):
            row = (my_col // ratio) ^ chip
            left = jnp.concatenate([lefts[chip * ratio + p][skip + s] for p in range(ratio)], axis=1)
            right = jnp.concatenate([held[row, p, s] for p in range(ratio)], axis=0)
            part = jnp.dot(left, right, preferred_element_type=jnp.float32)
            acc = part if acc is None else acc + part
        live = (base + s < my_count).astype(jnp.float32)
        total[...] = acc * live
        for step in range(ratio):
            part = core ^ step
            outs[step][s] = total[pl.ds(pl.multiple_of(part * half, half), half), :].astype(jnp.bfloat16)
        return 0

    lax.fori_loop(0, size, one, 0)


def collect(refs, held, sizes, ratio, core):
    base = 0
    for chunk, size in enumerate(sizes):
        for step in range(ratio):
            held[core ^ step, base : base + size] = refs[chunk * ratio + step][...]
        base += size


def summed(held_own, s, held_their, t, ratio):
    own = jnp.concatenate([held_own[p, s] for p in range(ratio)], axis=0).astype(jnp.float32)
    if t is None:
        return own
    return own + jnp.concatenate([held_their[p, t].astype(jnp.float32).T for p in range(ratio)], axis=0)


def final_kernel(ratio, sizes, list_ref, count_ref, *refs):
    slots = sum(sizes)
    early = sizes[0]
    owns = refs[: len(sizes) * ratio]
    theirs = refs[len(sizes) * ratio : -3]
    out_ref, held_own, held_their = refs[-3:]
    my_row = lax.axis_index("row")
    my_col = lax.axis_index("col")
    core = lax.rem(my_col, ratio)
    partner = my_col // ratio
    collect(owns, held_own, sizes, ratio, core)
    collect(theirs, held_their, sizes[:1], ratio, core)
    my_count = count_ref[my_row]
    depth = out_ref.shape[0]

    def one(s, _):
        first = list_ref[my_row, 0, s]
        second = list_ref[my_row, 1, s]
        found = jnp.int32(-1)
        for t in range(early):
            hit = (list_ref[partner, 0, t] == second) & (list_ref[partner, 1, t] == first)
            found = jnp.where(hit, t, found)
        use = (s < my_count) & (found >= 0)

        @pl.when(use)
        def _():
            x = summed(held_own, s, held_their, jnp.maximum(found, 0), ratio)
            out_ref[:, s] = swap(x).reshape(depth, TILE, LANES)

        @pl.when(jnp.logical_not(use))
        def _():
            x = summed(held_own, s, None, None, ratio)
            out_ref[:, s] = swap(x).reshape(depth, TILE, LANES)

        return 0

    lax.fori_loop(0, slots, one, 0)


def patch_kernel(ratio, sizes, list_ref, count_ref, *refs):
    slots = sum(sizes)
    early = sizes[0]
    owns = refs[: len(sizes) * ratio]
    theirs = refs[len(sizes) * ratio : -6]
    _, out_ref, held_own, held_their, built, sem = refs[-6:]
    my_row = lax.axis_index("row")
    my_col = lax.axis_index("col")
    core = lax.rem(my_col, ratio)
    partner = my_col // ratio
    collect(owns, held_own, sizes, ratio, core)
    collect(theirs, held_their, sizes[1:], ratio, core)
    my_count = count_ref[my_row]
    depth = out_ref.shape[0]
    uses, copies = [], []
    for t in range(slots - early):
        first = list_ref[partner, 0, early + t]
        second = list_ref[partner, 1, early + t]
        found = jnp.int32(-1)
        for s in range(slots):
            hit = (list_ref[my_row, 0, s] == second) & (list_ref[my_row, 1, s] == first)
            found = jnp.where(hit, s, found)
        uses.append((found < my_count) & (found >= 0))
        s = jnp.maximum(found, 0)
        copies.append(pltpu.make_async_copy(built.at[t], out_ref.at[:, s], sem.at[t]))

        @pl.when(uses[-1])
        def _(s=s, t=t):
            built[t] = swap(summed(held_own, s, held_their, t, ratio)).reshape(depth, TILE, LANES)
            copies[t].start()

    for use, copy in zip(uses, copies):
        pl.when(use)(copy.wait)


def mirror_pairs(rows, cols, step, hop):
    ratio = cols // rows
    pairs = []
    for row in range(rows):
        for col in range(cols):
            part = (col % ratio + step) % ratio
            held = col ^ hop
            pairs.append((row * cols + held, (col // ratio) * cols + row * ratio + part))
    return pairs


def on_device(amplitudes, integrals, pair_lists, tile_counts):
    rows = lax.axis_size("row")
    cols = lax.axis_size("col")
    ratio = cols // rows
    occ_row, occ_col, slots, square = amplitudes.shape
    assert occ_col * TILE == LANES and occ_row == ratio * occ_col
    assert ratio == 2 and rows & (rows - 1) == 0
    sizes = SPLIT if sum(SPLIT) == slots else (slots - 1, 1)
    tall = occ_row * TILE
    wide = occ_col * TILE
    lists = jnp.transpose(pair_lists, (0, 2, 1))
    bf16 = jnp.bfloat16

    table = rows_of(integrals)

    rights = []
    base = 0
    for size in sizes:
        picked = pl.pallas_call(
            functools.partial(pick_kernel, base, size, rows),
            out_shape=[jax.ShapeDtypeStruct((size, tall, wide), bf16)] * rows,
            in_specs=[SMEM, VMEM],
            out_specs=[VMEM] * rows,
            compiler_params=PARAMS,
            name="pick",
        )(lists, table)
        got = [picked[0]]
        for shift in range(1, rows):
            pairs = [(r, r ^ shift) for r in range(rows)]
            got.append(lax.ppermute(picked[shift], "row", pairs))
        rights.append(got)
        base += size

    parts = (sizes[0], slots - sizes[0])
    mine = pl.pallas_call(
        left_kernel,
        out_shape=[jax.ShapeDtypeStruct((n, tall, wide), bf16) for n in parts],
        in_specs=[VMEM],
        out_specs=[VMEM] * 2,
        compiler_params=PARAMS,
        name="left",
    )(rows_of(amplitudes))
    lefts = []
    for part in range(2):
        got = [mine[part]]
        for e in range(1, cols):
            source = got[e - 1] if e % 2 else got[0]
            step = 1 if e % 2 else e
            got.append(lax.ppermute(source, "col", [(c, c ^ step) for c in range(cols)]))
        lefts.append(got)

    owns, theirs = [], []
    base = 0
    for chunk, size in enumerate(sizes):
        sent = pl.pallas_call(
            functools.partial(cycle_kernel, rows, cols, ratio, base, base if chunk == 0 else base - sizes[0], size),
            out_shape=[jax.ShapeDtypeStruct((size, tall // ratio, wide), bf16)] * ratio,
            in_specs=[SMEM] + [VMEM] * (cols + rows),
            out_specs=[VMEM] * ratio,
            scratch_shapes=[
                pltpu.VMEM((rows, ratio, size, tall // ratio, wide), bf16),
                pltpu.VMEM((tall, wide), jnp.float32),
            ],
            compiler_params=PARAMS,
            name="cycle",
        )(tile_counts, *lefts[min(chunk, 1)], *rights[chunk])
        owns += sent
        for step in range(ratio):
            block = sent[step]
            way = HOPS[chunk][step]
            hop = (way & 1) * ratio + (way >> 1) * (cols // 2)
            if hop:
                block = lax.ppermute(block, "col", [(c, c ^ hop) for c in range(cols)])
            theirs.append(lax.ppermute(block, ("row", "col"), mirror_pairs(rows, cols, step, hop)))
        base += size

    out_shape = jax.ShapeDtypeStruct((occ_row, slots, square // LANES * occ_col, LANES), jnp.float32)
    block = (tall // ratio, wide)
    split = ratio
    late = slots - sizes[0]
    out = pl.pallas_call(
        functools.partial(final_kernel, ratio, sizes),
        out_shape=out_shape,
        in_specs=[SMEM, SMEM] + [VMEM] * (len(owns) + split),
        out_specs=VMEM,
        scratch_shapes=[
            pltpu.VMEM((ratio, slots) + block, bf16),
            pltpu.VMEM((ratio, sizes[0]) + block, bf16),
        ],
        compiler_params=PARAMS,
        name="final",
    )(lists, tile_counts, *owns, *theirs[:split])
    out = pl.pallas_call(
        functools.partial(patch_kernel, ratio, sizes),
        out_shape=out_shape,
        in_specs=[SMEM, SMEM] + [VMEM] * (len(owns) + len(theirs) - split) + [HBM],
        out_specs=HBM,
        scratch_shapes=[
            pltpu.VMEM((ratio, slots) + block, bf16),
            pltpu.VMEM((ratio, late) + block, bf16),
            pltpu.VMEM((late, occ_row, TILE, LANES), jnp.float32),
            pltpu.SemaphoreType.DMA((late,)),
        ],
        input_output_aliases={2 + len(owns) + len(theirs) - split: 0},
        compiler_params=PARAMS,
        name="patch",
    )(lists, tile_counts, *owns, *theirs[split:], out)
    return tiles_of(out, occ_col)


def solution(mesh):
    return jax.shard_map(
        on_device,
        mesh=mesh,
        in_specs=(P("row", "col", None, None), P("row", "col", None, None), P(), P()),
        out_specs=P("row", "col", None, None),
        check_vma=False,
    )
```

```python
import functools

import jax
import jax.numpy as jnp
from jax import lax
from jax.experimental import pallas as pl
from jax.experimental.pallas import tpu as pltpu
from jax.sharding import PartitionSpec as P


TILE = 64
LANES = 128
SPLIT = (6, 4, 2)
HOPS = ((1, 3), (0, 2), (0, 2))
VMEM = pl.BlockSpec(memory_space=pltpu.VMEM)
SMEM = pl.BlockSpec(memory_space=pltpu.SMEM)
HBM = pl.BlockSpec(memory_space=pltpu.HBM)
PARAMS = pltpu.CompilerParams(vmem_limit_bytes=16 * 1024 * 1024)


def rows_of(x):
    outer, pair, slots, square = x.shape
    x = jnp.transpose(x, (0, 2, 1, 3)).reshape(outer, slots, pair, square // LANES, LANES)
    return jnp.transpose(x, (0, 1, 3, 2, 4)).reshape(outer, slots, square // LANES * pair, LANES)


def tiles_of(x, pair):
    outer, slots, rows, lanes = x.shape
    x = x.reshape(outer, slots, rows // pair, pair, lanes)
    x = jnp.transpose(x, (0, 1, 3, 2, 4)).reshape(outer, slots, pair, rows // pair * lanes)
    return jnp.transpose(x, (0, 2, 1, 3))


def swap(x):
    count = x.shape[0]
    x = x.reshape(count // 8, 8, LANES)
    odd = lax.broadcasted_iota(jnp.int32, x.shape, 1) % 2
    half = lax.broadcasted_iota(jnp.int32, x.shape, 2) // TILE
    other = jnp.where(odd == 0, pltpu.roll(x, 7, 1), pltpu.roll(x, 1, 1))
    out = jnp.where(odd == half, x, pltpu.roll(other, TILE, 2))
    return out.reshape(count, LANES)


def pick_kernel(base, size, shifts, list_ref, w_ref, *outs):
    my_row = lax.axis_index("row")
    depth = w_ref.shape[0]
    for shift, out in zip(shifts, outs):
        row = my_row ^ shift

        def one(s, _, out=out, row=row):
            tile = list_ref[row, 1, base + s]
            x = w_ref[:, tile].reshape(depth * TILE, LANES).astype(jnp.float32)
            out[s] = swap(x).astype(jnp.bfloat16)
            return 0

        lax.fori_loop(0, size, one, 0, unroll=True)


def left_kernel(a_ref, *outs):
    depth = a_ref.shape[0]
    base = 0
    for out in outs:

        def one(s, _, out=out, base=base):
            x = a_ref[:, base + s].reshape(depth * TILE, LANES).astype(jnp.float32)
            out[s] = swap(x).astype(jnp.bfloat16)
            return 0

        lax.fori_loop(0, out.shape[0], one, 0, unroll=True)
        base += out.shape[0]


def cycle_kernel(rows, cols, ratio, base, skip, size, *refs):
    count_ref = refs[0]
    lefts = refs[1 : 1 + cols]
    rights = refs[1 + cols : 1 + cols + rows]
    outs = refs[1 + cols + rows : -2]
    held, total = refs[-2:]
    my_row = lax.axis_index("row")
    my_col = lax.axis_index("col")
    core = lax.rem(my_col, ratio)
    half = total.shape[1] // ratio
    for d, right in enumerate(rights):
        row = my_row ^ d
        for p in range(ratio):
            held[row, p] = right[:, pl.ds(pl.multiple_of((p ^ core) * half, half), half), :]
    my_count = count_ref[my_row]

    def one(s, _):
        acc = None
        for chip in range(rows):
            row = (my_col // ratio) ^ chip
            left = jnp.concatenate([lefts[chip * ratio + p][skip + s] for p in range(ratio)], axis=1)
            right = jnp.concatenate([held[row, p, s] for p in range(ratio)], axis=0)
            part = jnp.dot(left, right, preferred_element_type=jnp.float32)
            acc = part if acc is None else acc + part
        live = (base + s < my_count).astype(jnp.float32)
        total[s] = acc * live
        for step in range(ratio):
            part = core ^ step
            outs[step][s] = total[s, pl.ds(pl.multiple_of(part * half, half), half), :].astype(jnp.bfloat16)
        return 0

    lax.fori_loop(0, size, one, 0, unroll=True)


def collect(refs, held, sizes, ratio, core):
    base = 0
    for chunk, size in enumerate(sizes):
        for step in range(ratio):
            held[core ^ step, base : base + size] = refs[chunk * ratio + step][...]
        base += size


def summed(held_own, s, held_their, t, ratio):
    own = jnp.concatenate([held_own[p, s] for p in range(ratio)], axis=0).astype(jnp.float32)
    if t is None:
        return own
    return own + jnp.concatenate([held_their[p, t].astype(jnp.float32).T for p in range(ratio)], axis=0)


def final_kernel(ratio, sizes, list_ref, count_ref, *refs):
    slots = sum(sizes)
    early = sizes[0]
    owns = refs[: len(sizes) * ratio]
    theirs = refs[len(sizes) * ratio : -3]
    out_ref, table_ref, held_own, held_their = refs[-4:]
    my_row = lax.axis_index("row")
    my_col = lax.axis_index("col")
    core = lax.rem(my_col, ratio)
    partner = my_col // ratio
    collect(owns, held_own, sizes, ratio, core)
    collect(theirs, held_their, sizes[:1], ratio, core)
    my_count = count_ref[my_row]
    depth = out_ref.shape[0]

    for t in range(slots):
        table_ref[0, t] = -1

    def one(s, _):
        first = list_ref[my_row, 0, s]
        second = list_ref[my_row, 1, s]
        found = jnp.int32(-1)
        for t in range(slots):
            hit = (list_ref[partner, 0, t] == second) & (list_ref[partner, 1, t] == first)
            found = jnp.where(hit, t, found)
        use = (s < my_count) & (found >= 0)

        @pl.when(use)
        def _():
            table_ref[0, found] = s

        use = use & (found < early)

        @pl.when(use)
        def _():
            x = summed(held_own, s, held_their, jnp.where(use, found, 0), ratio)
            out_ref[:, s] = swap(x).reshape(depth, TILE, LANES)

        @pl.when(jnp.logical_not(use))
        def _():
            x = summed(held_own, s, None, None, ratio)
            out_ref[:, s] = swap(x).reshape(depth, TILE, LANES)

        return 0

    lax.fori_loop(0, slots, one, 0)


def patch_kernel(ratio, sizes, table_ref, *refs):
    slots = sum(sizes)
    early = sizes[0]
    owns = refs[: len(sizes) * ratio]
    theirs = refs[len(sizes) * ratio : -6]
    _, out_ref, held_own, held_their, built, sem = refs[-6:]
    core = lax.rem(lax.axis_index("col"), ratio)
    collect(owns, held_own, sizes, ratio, core)
    collect(theirs, held_their, sizes[1:], ratio, core)
    depth = out_ref.shape[0]
    uses, copies = [], []
    for t in range(slots - early):
        found = table_ref[0, early + t]
        uses.append(found >= 0)
        s = jnp.maximum(found, 0)
        copies.append(pltpu.make_async_copy(built.at[t], out_ref.at[:, s], sem.at[t]))

        @pl.when(uses[-1])
        def _(s=s, t=t):
            built[t] = swap(summed(held_own, s, held_their, t, ratio)).reshape(depth, TILE, LANES)
            copies[t].start()

    for use, copy in zip(uses, copies):
        pl.when(use)(copy.wait)


def mirror_pairs(rows, cols, step, hop):
    ratio = cols // rows
    pairs = []
    for row in range(rows):
        for col in range(cols):
            part = (col % ratio + step) % ratio
            held = col ^ hop
            pairs.append((row * cols + held, (col // ratio) * cols + row * ratio + part))
    return pairs


def on_device(amplitudes, integrals, pair_lists, tile_counts):
    rows = lax.axis_size("row")
    cols = lax.axis_size("col")
    ratio = cols // rows
    occ_row, occ_col, slots, square = amplitudes.shape
    assert occ_col * TILE == LANES and occ_row == ratio * occ_col
    assert ratio == 2 and rows & (rows - 1) == 0
    sizes = SPLIT if sum(SPLIT) == slots else (slots - 1, 1)
    tall = occ_row * TILE
    wide = occ_col * TILE
    lists = jnp.transpose(pair_lists, (0, 2, 1))
    bf16 = jnp.bfloat16

    tiles = rows_of(integrals)

    rights = []
    base = 0
    for chunk, size in enumerate(sizes):
        picked = {}
        far = rows - 1
        for shifts in ((far,), range(far)) if chunk == 0 else (range(rows),):
            new = pl.pallas_call(
                functools.partial(pick_kernel, base, size, tuple(shifts)),
                out_shape=[jax.ShapeDtypeStruct((size, tall, wide), bf16)] * len(shifts),
                in_specs=[SMEM, VMEM],
                out_specs=[VMEM] * len(shifts),
                compiler_params=PARAMS,
                name="pick",
            )(lists, tiles)
            picked.update(zip(shifts, new))
        got = [picked[0]]
        for shift in range(1, rows):
            pairs = [(r, r ^ shift) for r in range(rows)]
            got.append(lax.ppermute(picked[shift], "row", pairs))
        rights.append(got)
        base += size

    parts = (sizes[0], slots - sizes[0])
    mine = pl.pallas_call(
        left_kernel,
        out_shape=[jax.ShapeDtypeStruct((n, tall, wide), bf16) for n in parts],
        in_specs=[VMEM],
        out_specs=[VMEM] * 2,
        compiler_params=PARAMS,
        name="left",
    )(rows_of(amplitudes))
    lefts = []
    for part in range(2):
        got = [mine[part]]
        for e in range(1, cols):
            source = got[e - 1] if e % 2 else got[0]
            step = 1 if e % 2 else e
            got.append(lax.ppermute(source, "col", [(c, c ^ step) for c in range(cols)]))
        lefts.append(got)

    owns, theirs = [], []
    base = 0
    for chunk, size in enumerate(sizes):
        sent = pl.pallas_call(
            functools.partial(cycle_kernel, rows, cols, ratio, base, base if chunk == 0 else base - sizes[0], size),
            out_shape=[jax.ShapeDtypeStruct((size, tall // ratio, wide), bf16)] * ratio,
            in_specs=[SMEM] + [VMEM] * (cols + rows),
            out_specs=[VMEM] * ratio,
            scratch_shapes=[
                pltpu.VMEM((rows, ratio, size, tall // ratio, wide), bf16),
                pltpu.VMEM((size, tall, wide), jnp.float32),
            ],
            compiler_params=PARAMS,
            name="cycle",
        )(tile_counts, *lefts[min(chunk, 1)], *rights[chunk])
        owns += sent
        for step in range(ratio):
            block = sent[step]
            way = HOPS[chunk][step]
            hop = (way & 1) * ratio + (way >> 1) * (cols // 2)
            if hop:
                block = lax.ppermute(block, "col", [(c, c ^ hop) for c in range(cols)])
            theirs.append(lax.ppermute(block, ("row", "col"), mirror_pairs(rows, cols, step, hop)))
        base += size

    out_shape = jax.ShapeDtypeStruct((occ_row, slots, square // LANES * occ_col, LANES), jnp.float32)
    block = (tall // ratio, wide)
    split = ratio
    late = slots - sizes[0]
    out, table = pl.pallas_call(
        functools.partial(final_kernel, ratio, sizes),
        out_shape=[out_shape, jax.ShapeDtypeStruct((1, slots), jnp.int32)],
        in_specs=[SMEM, SMEM] + [VMEM] * (len(owns) + split),
        out_specs=[VMEM, SMEM],
        scratch_shapes=[
            pltpu.VMEM((ratio, slots) + block, bf16),
            pltpu.VMEM((ratio, sizes[0]) + block, bf16),
        ],
        compiler_params=PARAMS,
        name="final",
    )(lists, tile_counts, *owns, *theirs[:split])
    out = pl.pallas_call(
        functools.partial(patch_kernel, ratio, sizes),
        out_shape=out_shape,
        in_specs=[SMEM] + [VMEM] * (len(owns) + len(theirs) - split) + [HBM],
        out_specs=HBM,
        scratch_shapes=[
            pltpu.VMEM((ratio, slots) + block, bf16),
            pltpu.VMEM((ratio, late) + block, bf16),
            pltpu.VMEM((late, occ_row, TILE, LANES), jnp.float32),
            pltpu.SemaphoreType.DMA((late,)),
        ],
        input_output_aliases={1 + len(owns) + len(theirs) - split: 0},
        compiler_params=PARAMS,
        name="patch",
    )(table, *owns, *theirs[split:], out)
    return tiles_of(out, occ_col)


def solution(mesh):
    return jax.shard_map(
        on_device,
        mesh=mesh,
        in_specs=(P("row", "col", None, None), P("row", "col", None, None), P(), P()),
        out_specs=P("row", "col", None, None),
        check_vma=False,
    )
```

```python
import functools

import jax
import jax.numpy as jnp
from jax import lax
from jax.experimental import pallas as pl
from jax.experimental.pallas import tpu as pltpu
from jax.sharding import PartitionSpec as P


TILE = 64
LANES = 128
SPLIT = (6, 4, 2)
HOPS = ((1, 3), (0, 2), (0, 2))
VMEM = pl.BlockSpec(memory_space=pltpu.VMEM)
SMEM = pl.BlockSpec(memory_space=pltpu.SMEM)
HBM = pl.BlockSpec(memory_space=pltpu.HBM)
PARAMS = pltpu.CompilerParams(vmem_limit_bytes=16 * 1024 * 1024)


def rows_of(x):
    outer, pair, slots, square = x.shape
    x = jnp.transpose(x, (0, 2, 1, 3)).reshape(outer, slots, pair, square // LANES, LANES)
    return jnp.transpose(x, (0, 1, 3, 2, 4)).reshape(outer, slots, square // LANES * pair, LANES)


def tiles_of(x, pair):
    outer, slots, rows, lanes = x.shape
    x = x.reshape(outer, slots, rows // pair, pair, lanes)
    x = jnp.transpose(x, (0, 1, 3, 2, 4)).reshape(outer, slots, pair, rows // pair * lanes)
    return jnp.transpose(x, (0, 2, 1, 3))


def swap(x):
    count = x.shape[0]
    x = x.reshape(count // 8, 8, LANES)
    odd = lax.broadcasted_iota(jnp.int32, x.shape, 1) % 2
    half = lax.broadcasted_iota(jnp.int32, x.shape, 2) // TILE
    other = jnp.where(odd == 0, pltpu.roll(x, 7, 1), pltpu.roll(x, 1, 1))
    out = jnp.where(odd == half, x, pltpu.roll(other, TILE, 2))
    return out.reshape(count, LANES)


def pick_kernel(base, size, shifts, list_ref, w_ref, *outs):
    my_row = lax.axis_index("row")
    depth = w_ref.shape[0]
    for shift, out in zip(shifts, outs):
        row = my_row ^ shift

        def one(s, _, out=out, row=row):
            tile = list_ref[row, 1, base + s]
            x = w_ref[:, tile].reshape(depth * TILE, LANES).astype(jnp.float32)
            out[s] = swap(x).astype(jnp.bfloat16)
            return 0

        lax.fori_loop(0, size, one, 0, unroll=True)


def left_kernel(a_ref, *outs):
    depth = a_ref.shape[0]
    base = 0
    for out in outs:

        def one(s, _, out=out, base=base):
            x = a_ref[:, base + s].reshape(depth * TILE, LANES).astype(jnp.float32)
            out[s] = swap(x).astype(jnp.bfloat16)
            return 0

        lax.fori_loop(0, out.shape[0], one, 0, unroll=True)
        base += out.shape[0]


def cycle_kernel(rows, cols, ratio, base, skip, size, *refs):
    count_ref = refs[0]
    lefts = refs[1 : 1 + cols]
    rights = refs[1 + cols : 1 + cols + rows]
    outs = refs[1 + cols + rows : -2]
    held, total = refs[-2:]
    my_row = lax.axis_index("row")
    my_col = lax.axis_index("col")
    core = lax.rem(my_col, ratio)
    half = total.shape[1] // ratio
    for d, right in enumerate(rights):
        row = my_row ^ d
        for p in range(ratio):
            held[row, p] = right[:, pl.ds(pl.multiple_of((p ^ core) * half, half), half), :]
    my_count = count_ref[my_row]

    def one(s, _):
        acc = None
        for chip in range(rows):
            row = (my_col // ratio) ^ chip
            left = jnp.concatenate([lefts[chip * ratio + p][skip + s] for p in range(ratio)], axis=1)
            right = jnp.concatenate([held[row, p, s] for p in range(ratio)], axis=0)
            part = jnp.dot(left, right, preferred_element_type=jnp.float32)
            acc = part if acc is None else acc + part
        live = (base + s < my_count).astype(jnp.float32)
        total[s] = acc * live
        for step in range(ratio):
            part = core ^ step
            outs[step][s] = total[s, pl.ds(pl.multiple_of(part * half, half), half), :].astype(jnp.bfloat16)
        return 0

    lax.fori_loop(0, size, one, 0, unroll=True)


def collect(refs, held, sizes, ratio, core):
    base = 0
    for chunk, size in enumerate(sizes):
        for step in range(ratio):
            held[core ^ step, base : base + size] = refs[chunk * ratio + step][...]
        base += size


def summed(held_own, s, held_their, t, ratio):
    own = jnp.concatenate([held_own[p, s] for p in range(ratio)], axis=0).astype(jnp.float32)
    if t is None:
        return own
    return own + jnp.concatenate([held_their[p, t].astype(jnp.float32).T for p in range(ratio)], axis=0)


def final_kernel(ratio, sizes, list_ref, count_ref, *refs):
    slots = sum(sizes)
    early = sizes[0]
    owns = refs[: len(sizes) * ratio]
    theirs = refs[len(sizes) * ratio : -3]
    out_ref, table_ref, held_own, held_their = refs[-4:]
    my_row = lax.axis_index("row")
    my_col = lax.axis_index("col")
    core = lax.rem(my_col, ratio)
    partner = my_col // ratio
    collect(owns, held_own, sizes, ratio, core)
    collect(theirs, held_their, sizes[:1], ratio, core)
    my_count = count_ref[my_row]
    depth = out_ref.shape[0]

    for t in range(slots):
        table_ref[0, t] = -1

    def one(s, _):
        first = list_ref[my_row, 0, s]
        second = list_ref[my_row, 1, s]
        found = jnp.int32(-1)
        for t in range(slots):
            hit = (list_ref[partner, 0, t] == second) & (list_ref[partner, 1, t] == first)
            found = jnp.where(hit, t, found)
        use = (s < my_count) & (found >= 0)

        @pl.when(use)
        def _():
            table_ref[0, found] = s

        use = use & (found < early)

        @pl.when(use)
        def _():
            x = summed(held_own, s, held_their, jnp.where(use, found, 0), ratio)
            out_ref[:, s] = swap(x).reshape(depth, TILE, LANES)

        @pl.when(jnp.logical_not(use))
        def _():
            x = summed(held_own, s, None, None, ratio)
            out_ref[:, s] = swap(x).reshape(depth, TILE, LANES)

        return 0

    lax.fori_loop(0, slots, one, 0)


def patch_kernel(ratio, sizes, chunk, table_ref, *refs):
    early = sum(sizes[:chunk])
    owns = refs[: len(sizes) * ratio]
    theirs = refs[len(sizes) * ratio : -6]
    _, out_ref, held_own, held_their, built, sem = refs[-6:]
    core = lax.rem(lax.axis_index("col"), ratio)
    collect(owns, held_own, sizes, ratio, core)
    collect(theirs, held_their, sizes[chunk : chunk + 1], ratio, core)
    depth = out_ref.shape[0]
    uses, copies = [], []
    for t in range(sizes[chunk]):
        found = table_ref[0, early + t]
        uses.append(found >= 0)
        s = jnp.maximum(found, 0)
        copies.append(pltpu.make_async_copy(built.at[t], out_ref.at[:, s], sem.at[t]))

        @pl.when(uses[-1])
        def _(s=s, t=t):
            built[t] = swap(summed(held_own, s, held_their, t, ratio)).reshape(depth, TILE, LANES)
            copies[t].start()

    for use, copy in zip(uses, copies):
        pl.when(use)(copy.wait)


def mirror_pairs(rows, cols, step, hop):
    ratio = cols // rows
    pairs = []
    for row in range(rows):
        for col in range(cols):
            part = (col % ratio + step) % ratio
            held = col ^ hop
            pairs.append((row * cols + held, (col // ratio) * cols + row * ratio + part))
    return pairs


def on_device(amplitudes, integrals, pair_lists, tile_counts):
    rows = lax.axis_size("row")
    cols = lax.axis_size("col")
    ratio = cols // rows
    occ_row, occ_col, slots, square = amplitudes.shape
    assert occ_col * TILE == LANES and occ_row == ratio * occ_col
    assert ratio == 2 and rows & (rows - 1) == 0
    sizes = SPLIT if sum(SPLIT) == slots else (slots - 1, 1)
    tall = occ_row * TILE
    wide = occ_col * TILE
    lists = jnp.transpose(pair_lists, (0, 2, 1))
    bf16 = jnp.bfloat16

    tiles = rows_of(integrals)

    rights = []
    base = 0
    for chunk, size in enumerate(sizes):
        picked = {}
        far = rows - 1
        for shifts in ((far,), range(far)) if chunk == 0 else (range(rows),):
            new = pl.pallas_call(
                functools.partial(pick_kernel, base, size, tuple(shifts)),
                out_shape=[jax.ShapeDtypeStruct((size, tall, wide), bf16)] * len(shifts),
                in_specs=[SMEM, VMEM],
                out_specs=[VMEM] * len(shifts),
                compiler_params=PARAMS,
                name="pick",
            )(lists, tiles)
            picked.update(zip(shifts, new))
        got = [picked[0]]
        for shift in range(1, rows):
            pairs = [(r, r ^ shift) for r in range(rows)]
            got.append(lax.ppermute(picked[shift], "row", pairs))
        rights.append(got)
        base += size

    parts = (sizes[0], slots - sizes[0])
    mine = pl.pallas_call(
        left_kernel,
        out_shape=[jax.ShapeDtypeStruct((n, tall, wide), bf16) for n in parts],
        in_specs=[VMEM],
        out_specs=[VMEM] * 2,
        compiler_params=PARAMS,
        name="left",
    )(rows_of(amplitudes))
    lefts = []
    for part in range(2):
        got = [mine[part]]
        for e in range(1, cols):
            source = got[e - 1] if e % 2 else got[0]
            step = 1 if e % 2 else e
            got.append(lax.ppermute(source, "col", [(c, c ^ step) for c in range(cols)]))
        lefts.append(got)

    owns, theirs = [], []
    base = 0
    for chunk, size in enumerate(sizes):
        sent = pl.pallas_call(
            functools.partial(cycle_kernel, rows, cols, ratio, base, base if chunk == 0 else base - sizes[0], size),
            out_shape=[jax.ShapeDtypeStruct((size, tall // ratio, wide), bf16)] * ratio,
            in_specs=[SMEM] + [VMEM] * (cols + rows),
            out_specs=[VMEM] * ratio,
            scratch_shapes=[
                pltpu.VMEM((rows, ratio, size, tall // ratio, wide), bf16),
                pltpu.VMEM((size, tall, wide), jnp.float32),
            ],
            compiler_params=PARAMS,
            name="cycle",
        )(tile_counts, *lefts[min(chunk, 1)], *rights[chunk])
        owns += sent
        for step in range(ratio):
            block = sent[step]
            way = HOPS[chunk][step]
            hop = (way & 1) * ratio + (way >> 1) * (cols // 2)
            if hop:
                block = lax.ppermute(block, "col", [(c, c ^ hop) for c in range(cols)])
            theirs.append(lax.ppermute(block, ("row", "col"), mirror_pairs(rows, cols, step, hop)))
        base += size

    out_shape = jax.ShapeDtypeStruct((occ_row, slots, square // LANES * occ_col, LANES), jnp.float32)
    block = (tall // ratio, wide)
    split = ratio
    out, table = pl.pallas_call(
        functools.partial(final_kernel, ratio, sizes),
        out_shape=[out_shape, jax.ShapeDtypeStruct((1, slots), jnp.int32)],
        in_specs=[SMEM, SMEM] + [VMEM] * (len(owns) + split),
        out_specs=[VMEM, SMEM],
        scratch_shapes=[
            pltpu.VMEM((ratio, slots) + block, bf16),
            pltpu.VMEM((ratio, sizes[0]) + block, bf16),
        ],
        compiler_params=PARAMS,
        name="final",
    )(lists, tile_counts, *owns, *theirs[:split])
    for chunk in range(1, len(sizes)):
        late = sizes[chunk]
        out = pl.pallas_call(
            functools.partial(patch_kernel, ratio, sizes, chunk),
            out_shape=out_shape,
            in_specs=[SMEM] + [VMEM] * (len(owns) + ratio) + [HBM],
            out_specs=HBM,
            scratch_shapes=[
                pltpu.VMEM((ratio, slots) + block, bf16),
                pltpu.VMEM((ratio, late) + block, bf16),
                pltpu.VMEM((late, occ_row, TILE, LANES), jnp.float32),
                pltpu.SemaphoreType.DMA((late,)),
            ],
            input_output_aliases={1 + len(owns) + ratio: 0},
            compiler_params=PARAMS,
            name="patch",
        )(table, *owns, *theirs[ratio * chunk : ratio * (chunk + 1)], out)
    return tiles_of(out, occ_col)


def solution(mesh):
    return jax.shard_map(
        on_device,
        mesh=mesh,
        in_specs=(P("row", "col", None, None), P("row", "col", None, None), P(), P()),
        out_specs=P("row", "col", None, None),
        check_vma=False,
    )
```

```python
import functools

import jax
import jax.numpy as jnp
from jax import lax
from jax.experimental import pallas as pl
from jax.experimental.pallas import tpu as pltpu
from jax.sharding import PartitionSpec as P


TILE = 64
LANES = 128
SPLIT = (7, 3, 2)
HOPS = ((1, 3), (0, 2), (0, 2))
VMEM = pl.BlockSpec(memory_space=pltpu.VMEM)
SMEM = pl.BlockSpec(memory_space=pltpu.SMEM)
HBM = pl.BlockSpec(memory_space=pltpu.HBM)
PARAMS = pltpu.CompilerParams(vmem_limit_bytes=16 * 1024 * 1024)


def rows_of(x):
    outer, pair, slots, square = x.shape
    x = jnp.transpose(x, (0, 2, 1, 3)).reshape(outer, slots, pair, square // LANES, LANES)
    return jnp.transpose(x, (0, 1, 3, 2, 4)).reshape(outer, slots, square // LANES * pair, LANES)


def tiles_of(x, pair):
    outer, slots, rows, lanes = x.shape
    x = x.reshape(outer, slots, rows // pair, pair, lanes)
    x = jnp.transpose(x, (0, 1, 3, 2, 4)).reshape(outer, slots, pair, rows // pair * lanes)
    return jnp.transpose(x, (0, 2, 1, 3))


def swap(x):
    count = x.shape[0]
    x = x.reshape(count // 8, 8, LANES)
    odd = lax.broadcasted_iota(jnp.int32, x.shape, 1) % 2
    half = lax.broadcasted_iota(jnp.int32, x.shape, 2) // TILE
    other = jnp.where(odd == 0, pltpu.roll(x, 7, 1), pltpu.roll(x, 1, 1))
    out = jnp.where(odd == half, x, pltpu.roll(other, TILE, 2))
    return out.reshape(count, LANES)


def pick_kernel(base, size, shifts, list_ref, w_ref, *outs):
    my_row = lax.axis_index("row")
    depth = w_ref.shape[0]
    for shift, out in zip(shifts, outs):
        row = my_row ^ shift

        def one(s, _, out=out, row=row):
            tile = list_ref[row, 1, base + s]
            x = w_ref[:, tile].reshape(depth * TILE, LANES).astype(jnp.float32)
            out[s] = swap(x).astype(jnp.bfloat16)
            return 0

        lax.fori_loop(0, size, one, 0, unroll=True)


def left_kernel(a_ref, *outs):
    depth = a_ref.shape[0]
    base = 0
    for out in outs:

        def one(s, _, out=out, base=base):
            x = a_ref[:, base + s].reshape(depth * TILE, LANES).astype(jnp.float32)
            out[s] = swap(x).astype(jnp.bfloat16)
            return 0

        lax.fori_loop(0, out.shape[0], one, 0, unroll=True)
        base += out.shape[0]


def cycle_kernel(rows, cols, ratio, base, skip, size, *refs):
    count_ref = refs[0]
    lefts = refs[1 : 1 + cols]
    rights = refs[1 + cols : 1 + cols + rows]
    outs = refs[1 + cols + rows : -2]
    held, total = refs[-2:]
    my_row = lax.axis_index("row")
    my_col = lax.axis_index("col")
    core = lax.rem(my_col, ratio)
    half = total.shape[1] // ratio
    for d, right in enumerate(rights):
        row = my_row ^ d
        for p in range(ratio):
            held[row, p] = right[:, pl.ds(pl.multiple_of((p ^ core) * half, half), half), :]
    my_count = count_ref[my_row]

    def one(s, _):
        acc = None
        for chip in range(rows):
            row = (my_col // ratio) ^ chip
            left = jnp.concatenate([lefts[chip * ratio + p][skip + s] for p in range(ratio)], axis=1)
            right = jnp.concatenate([held[row, p, s] for p in range(ratio)], axis=0)
            part = jnp.dot(left, right, preferred_element_type=jnp.float32)
            acc = part if acc is None else acc + part
        live = (base + s < my_count).astype(jnp.float32)
        total[s] = acc * live
        for step in range(ratio):
            part = core ^ step
            outs[step][s] = total[s, pl.ds(pl.multiple_of(part * half, half), half), :].astype(jnp.bfloat16)
        return 0

    lax.fori_loop(0, size, one, 0, unroll=True)


def collect(refs, held, sizes, ratio, core):
    base = 0
    for chunk, size in enumerate(sizes):
        for step in range(ratio):
            held[core ^ step, base : base + size] = refs[chunk * ratio + step][...]
        base += size


def summed(held_own, s, held_their, t, ratio):
    own = jnp.concatenate([held_own[p, s] for p in range(ratio)], axis=0).astype(jnp.float32)
    if t is None:
        return own
    return own + jnp.concatenate([held_their[p, t].astype(jnp.float32).T for p in range(ratio)], axis=0)


def match_kernel(list_ref, count_ref, table_ref):
    slots = table_ref.shape[1]
    my_row = lax.axis_index("row")
    partner = lax.axis_index("col") // (lax.axis_size("col") // lax.axis_size("row"))
    my_count = count_ref[my_row]
    for t in range(slots):
        table_ref[1, t] = -1

    def one(s, _):
        first = list_ref[my_row, 0, s]
        second = list_ref[my_row, 1, s]
        found = jnp.int32(-1)
        for t in range(slots):
            hit = (list_ref[partner, 0, t] == second) & (list_ref[partner, 1, t] == first)
            found = jnp.where(hit, t, found)
        found = jnp.where(s < my_count, found, -1)
        table_ref[0, s] = found

        @pl.when(found >= 0)
        def _():
            table_ref[1, found] = s

        return 0

    lax.fori_loop(0, slots, one, 0)


def begin_kernel(ratio, sizes, *refs):
    owns = refs[:ratio]
    out_ref, held_own, built, sem = refs[ratio:]
    collect(owns, held_own, sizes[:1], ratio, lax.rem(lax.axis_index("col"), ratio))
    copies = []
    for s in range(sizes[0]):
        built[s] = swap(summed(held_own, s, None, None, ratio)).reshape(built.shape[1:])
        copies.append(pltpu.make_async_copy(built.at[s], out_ref.at[:, s], sem.at[s]))
        copies[s].start()
    for copy in copies:
        copy.wait()


def final_kernel(ratio, sizes, table_ref, *refs):
    slots = sum(sizes)
    early = sizes[0]
    owns = refs[: len(sizes) * ratio]
    theirs = refs[len(sizes) * ratio : -6]
    _, out_ref, held_own, held_their, built, sem = refs[-6:]
    core = lax.rem(lax.axis_index("col"), ratio)
    collect(owns, held_own, sizes, ratio, core)
    collect(theirs, held_their, sizes[:1], ratio, core)
    needs, copies = [], []
    for s in range(slots):
        found = table_ref[0, s]
        use = (found >= 0) & (found < early)
        needs.append(use if s < early else None)
        copies.append(pltpu.make_async_copy(built.at[s], out_ref.at[:, s], sem.at[s]))

        @pl.when(use)
        def _(s=s, found=found, use=use):
            x = summed(held_own, s, held_their, jnp.where(use, found, 0), ratio)
            built[s] = swap(x).reshape(built.shape[1:])

        if s >= early:

            @pl.when(jnp.logical_not(use))
            def _(s=s):
                built[s] = swap(summed(held_own, s, None, None, ratio)).reshape(built.shape[1:])

            copies[s].start()
        else:
            pl.when(use)(copies[s].start)
    for need, copy in zip(needs, copies):
        if need is None:
            copy.wait()
        else:
            pl.when(need)(copy.wait)


def patch_kernel(ratio, sizes, chunk, table_ref, *refs):
    early = sum(sizes[:chunk])
    owns = refs[: len(sizes) * ratio]
    theirs = refs[len(sizes) * ratio : -6]
    _, out_ref, held_own, held_their, built, sem = refs[-6:]
    core = lax.rem(lax.axis_index("col"), ratio)
    collect(owns, held_own, sizes, ratio, core)
    collect(theirs, held_their, sizes[chunk : chunk + 1], ratio, core)
    depth = out_ref.shape[0]
    uses, copies = [], []
    for t in range(sizes[chunk]):
        found = table_ref[1, early + t]
        uses.append(found >= 0)
        s = jnp.maximum(found, 0)
        copies.append(pltpu.make_async_copy(built.at[t], out_ref.at[:, s], sem.at[t]))

        @pl.when(uses[-1])
        def _(s=s, t=t):
            built[t] = swap(summed(held_own, s, held_their, t, ratio)).reshape(depth, TILE, LANES)
            copies[t].start()

    for use, copy in zip(uses, copies):
        pl.when(use)(copy.wait)


def mirror_pairs(rows, cols, step, hop):
    ratio = cols // rows
    pairs = []
    for row in range(rows):
        for col in range(cols):
            part = (col % ratio + step) % ratio
            held = col ^ hop
            pairs.append((row * cols + held, (col // ratio) * cols + row * ratio + part))
    return pairs


def on_device(amplitudes, integrals, pair_lists, tile_counts):
    rows = lax.axis_size("row")
    cols = lax.axis_size("col")
    ratio = cols // rows
    occ_row, occ_col, slots, square = amplitudes.shape
    assert occ_col * TILE == LANES and occ_row == ratio * occ_col
    assert ratio == 2 and rows & (rows - 1) == 0
    sizes = SPLIT if sum(SPLIT) == slots else (slots - 1, 1)
    tall = occ_row * TILE
    wide = occ_col * TILE
    lists = jnp.transpose(pair_lists, (0, 2, 1))
    bf16 = jnp.bfloat16

    tiles = rows_of(integrals)

    rights = []
    base = 0
    for chunk, size in enumerate(sizes):
        picked = {}
        far = rows - 1
        for shifts in ((far,), range(far)) if chunk == 0 else (range(rows),):
            new = pl.pallas_call(
                functools.partial(pick_kernel, base, size, tuple(shifts)),
                out_shape=[jax.ShapeDtypeStruct((size, tall, wide), bf16)] * len(shifts),
                in_specs=[SMEM, VMEM],
                out_specs=[VMEM] * len(shifts),
                compiler_params=PARAMS,
                name="pick",
            )(lists, tiles)
            picked.update(zip(shifts, new))
        got = [picked[0]]
        for shift in range(1, rows):
            pairs = [(r, r ^ shift) for r in range(rows)]
            got.append(lax.ppermute(picked[shift], "row", pairs))
        rights.append(got)
        base += size

    parts = (sizes[0], slots - sizes[0])
    mine = pl.pallas_call(
        left_kernel,
        out_shape=[jax.ShapeDtypeStruct((n, tall, wide), bf16) for n in parts],
        in_specs=[VMEM],
        out_specs=[VMEM] * 2,
        compiler_params=PARAMS,
        name="left",
    )(rows_of(amplitudes))
    lefts = []
    for part in range(2):
        got = [mine[part]]
        for e in range(1, cols):
            source = got[e - 1] if e % 2 else got[0]
            step = 1 if e % 2 else e
            got.append(lax.ppermute(source, "col", [(c, c ^ step) for c in range(cols)]))
        lefts.append(got)

    owns, theirs = [], []
    base = 0
    for chunk, size in enumerate(sizes):
        sent = pl.pallas_call(
            functools.partial(cycle_kernel, rows, cols, ratio, base, base if chunk == 0 else base - sizes[0], size),
            out_shape=[jax.ShapeDtypeStruct((size, tall // ratio, wide), bf16)] * ratio,
            in_specs=[SMEM] + [VMEM] * (cols + rows),
            out_specs=[VMEM] * ratio,
            scratch_shapes=[
                pltpu.VMEM((rows, ratio, size, tall // ratio, wide), bf16),
                pltpu.VMEM((size, tall, wide), jnp.float32),
            ],
            compiler_params=PARAMS,
            name="cycle",
        )(tile_counts, *lefts[min(chunk, 1)], *rights[chunk])
        owns += sent
        for step in range(ratio):
            block = sent[step]
            way = HOPS[chunk][step]
            hop = (way & 1) * ratio + (way >> 1) * (cols // 2)
            if hop:
                block = lax.ppermute(block, "col", [(c, c ^ hop) for c in range(cols)])
            theirs.append(lax.ppermute(block, ("row", "col"), mirror_pairs(rows, cols, step, hop)))
        base += size

    out_shape = jax.ShapeDtypeStruct((occ_row, slots, square // LANES * occ_col, LANES), jnp.float32)
    block = (tall // ratio, wide)
    split = ratio
    table = pl.pallas_call(
        match_kernel,
        out_shape=jax.ShapeDtypeStruct((2, slots), jnp.int32),
        in_specs=[SMEM, SMEM],
        out_specs=SMEM,
        compiler_params=PARAMS,
        name="match",
    )(lists, tile_counts)
    out = pl.pallas_call(
        functools.partial(begin_kernel, ratio, sizes),
        out_shape=out_shape,
        in_specs=[VMEM] * ratio,
        out_specs=HBM,
        scratch_shapes=[
            pltpu.VMEM((ratio, sizes[0]) + block, bf16),
            pltpu.VMEM((sizes[0], occ_row, TILE, LANES), jnp.float32),
            pltpu.SemaphoreType.DMA((sizes[0],)),
        ],
        compiler_params=PARAMS,
        name="begin",
    )(*owns[:ratio])
    out = pl.pallas_call(
        functools.partial(final_kernel, ratio, sizes),
        out_shape=out_shape,
        in_specs=[SMEM] + [VMEM] * (len(owns) + split) + [HBM],
        out_specs=HBM,
        scratch_shapes=[
            pltpu.VMEM((ratio, slots) + block, bf16),
            pltpu.VMEM((ratio, sizes[0]) + block, bf16),
            pltpu.VMEM((slots, occ_row, TILE, LANES), jnp.float32),
            pltpu.SemaphoreType.DMA((slots,)),
        ],
        input_output_aliases={1 + len(owns) + split: 0},
        compiler_params=PARAMS,
        name="final",
    )(table, *owns, *theirs[:split], out)
    for chunk in range(1, len(sizes)):
        late = sizes[chunk]
        out = pl.pallas_call(
            functools.partial(patch_kernel, ratio, sizes, chunk),
            out_shape=out_shape,
            in_specs=[SMEM] + [VMEM] * (len(owns) + ratio) + [HBM],
            out_specs=HBM,
            scratch_shapes=[
                pltpu.VMEM((ratio, slots) + block, bf16),
                pltpu.VMEM((ratio, late) + block, bf16),
                pltpu.VMEM((late, occ_row, TILE, LANES), jnp.float32),
                pltpu.SemaphoreType.DMA((late,)),
            ],
            input_output_aliases={1 + len(owns) + ratio: 0},
            compiler_params=PARAMS,
            name="patch",
        )(table, *owns, *theirs[ratio * chunk : ratio * (chunk + 1)], out)
    return tiles_of(out, occ_col)


def solution(mesh):
    return jax.shard_map(
        on_device,
        mesh=mesh,
        in_specs=(P("row", "col", None, None), P("row", "col", None, None), P(), P()),
        out_specs=P("row", "col", None, None),
        check_vma=False,
    )
```
